32 devices in a mesh: row: 4 (over y, x), col: 8 (over z, core).
Axes of the slice: x: 2, y: 2, z: 4, core: 2. Of those that a mesh axis runs over, the one named last changes fastest.
Arguments:
- query_acts: bfloat16 [2048, 6144], P('col', 'row'), may hold values from -6 to 6
- query_grads: bfloat16 [2048, 6144], P('row', 'col'), may hold values from -6 to 6
- act_basis: bfloat16 [6144, 6144], P('row', 'col'), may hold values from -0.078125 to 0.078125
- grad_basis: bfloat16 [6144, 6144], P('col', 'row'), may hold values from -0.078125 to 0.078125
- eigenvalues: float32 [6144, 6144], P('row', 'col'), may hold values from 0.05 to 5
- train_acts: bfloat16 [640, 6144], P('row', 'col'), may hold values from -6 to 6
- train_grads: bfloat16 [640, 6144], P('col', 'row'), may hold values from -6 to 6
Outputs:
- scores: float32 [8, 640], P(None, ('row', 'col'))
The draws below stay inside these ranges and needn't reach their ends.
All inputs are finite; a program needn't handle non-finite values.
Results may differ from the reference program's by a relative error of at most 0.012.
Values may be sent and summed in bfloat16 or wider, within the bound.
No kernel may reach another device: no remote copies, remote signals or barrier semaphores. Data moves between devices by JAX's collectives and lax.ppermute only.
A program may use at most 128 MiB of HBM per device.

```python
import math
import jax
import jax.numpy as jnp
from jax import lax

D = 6144
QUERIES = 8
QUERY_LEN = 256
QUERY_TOKENS = 2048
TRAIN_TOKENS = 640


def scaled_rows(key, salt, rows, cols):
    inner = jax.random.fold_in(key, salt)
    first = jax.random.fold_in(inner, 0)
    values = jax.random.truncated_normal(first, -4.0, 4.0, (rows, cols), jnp.float32)
    return values.astype(jnp.bfloat16)


def draw_query_acts(key, part):
    return scaled_rows(key, 101, QUERY_TOKENS, D)


def draw_query_grads(key, part):
    return scaled_rows(key, 202, QUERY_TOKENS, D)


def draw_train_acts(key, part):
    return scaled_rows(key, 303, TRAIN_TOKENS, D)


def draw_train_grads(key, part):
    return scaled_rows(key, 404, TRAIN_TOKENS, D)


def level_of(own_key, shape, cuts, least, top_value):
    def one(dim, shards_of):
        steps = jax.random.uniform(jax.random.fold_in(jax.random.fold_in(own_key, 6), dim), (shards_of,), jnp.float32, least / len(cuts), top_value / len(cuts))
        return jnp.repeat(jnp.exp(steps), shape[dim] // shards_of).reshape((-1,) + (1,) * (len(shape) - dim - 1))

    factor_of = one(*cuts[0])
    for cut in cuts[1:]:
        factor_of = factor_of * one(*cut)
    return factor_of


def noise(rng, dims, scale, reach, pieces=(), kind=jnp.bfloat16):
    entries = jax.random.normal(rng, dims, jnp.float32) * scale
    if len(pieces) > 0:
        entries = level_of(rng, dims, pieces, -0.22, 0.18) * entries
    return jnp.clip(entries, min=-reach, max=reach).astype(kind)


def setup_inputs(seed: int = 0) -> dict:
    splits = jax.random.split(jax.random.key(seed), 8)
    query_acts = draw_query_acts(jax.random.fold_in(splits[7], 71), 0)
    query_grads = draw_query_grads(jax.random.fold_in(splits[7], 71), 0)
    act_basis = noise(splits[2], (D, D), D ** -0.5, 0.078125, ((0, 4), (1, 8)))
    grad_basis = noise(splits[3], (D, D), D ** -0.5, 0.078125, ((0, 8), (1, 4)))
    eigenvalues = jnp.clip(jnp.exp(math.log(5.0) - 4.6051702 * jax.random.uniform(splits[4], (D, D), jnp.float32) ** level_of(splits[4], (D, D), ((0, 4), (1, 8)), -0.2, 0.2)), 0.05, 5.0)
    train_acts = draw_train_acts(jax.random.fold_in(splits[7], 71), 0)
    train_grads = draw_train_grads(jax.random.fold_in(splits[7], 71), 0)
    return dict(query_acts=query_acts, query_grads=query_grads, act_basis=act_basis, grad_basis=grad_basis, eigenvalues=eigenvalues, train_acts=train_acts, train_grads=train_grads)


damping = 0.01


def reference(query_acts, query_grads, act_basis, grad_basis, eigenvalues, train_acts, train_grads):
    rot_acts = jnp.dot(query_acts, act_basis, preferred_element_type=jnp.float32).astype(jnp.bfloat16)
    rot_grads = jnp.dot(query_grads, grad_basis, preferred_element_type=jnp.float32).astype(jnp.bfloat16)

    def one_query(index):
        start = (index * QUERY_LEN).astype(jnp.int32)
        grads_q = lax.dynamic_slice_in_dim(rot_grads, start, QUERY_LEN, 0)
        acts_q = lax.dynamic_slice_in_dim(rot_acts, start, QUERY_LEN, 0)
        outer = jnp.dot(grads_q.T, acts_q, preferred_element_type=jnp.float32)
        panel = (outer / (QUERY_LEN * (eigenvalues + damping))).astype(jnp.bfloat16)
        mapped = jnp.dot(train_acts, panel.T, preferred_element_type=jnp.float32)
        return jnp.sum(mapped * train_grads.astype(jnp.float32), axis=1) / D

    return lax.map(one_query, jnp.arange(QUERIES, dtype=jnp.int32))
```

```python
import jax
import jax.numpy as jnp
from jax import lax
from jax.experimental import pallas as pl
from jax.experimental.pallas import tpu as pltpu
from jax.sharding import PartitionSpec as P

D = 6144
QUERY_LEN = 256
damping = 0.01


BF = jnp.bfloat16
F32 = jnp.float32


def choose(index, options):
    out = options[-1]
    for k in range(len(options) - 2, -1, -1):
        if options[k] is not out:
            out = jnp.where(index == k, options[k], out)
    return out


def panel_kernel(rg_ref, ra_ref, inv_own_ref, inv_oth_ref, tg_ref, ta_own_ref, ta_oth_ref, out_ref):
    @pl.when(pl.program_id(0) == 0)
    def _():
        out_ref[...] = jnp.zeros_like(out_ref)

    half = inv_own_ref.shape[1]
    mapped = None
    for k, (inv, ta) in enumerate(((inv_own_ref, ta_own_ref), (inv_oth_ref, ta_oth_ref))):
        outer = lax.dot_general(
            rg_ref[...],
            ra_ref[:, k * half : (k + 1) * half],
            (((0,), (0,)), ((), ())),
            preferred_element_type=F32,
        )
        panel = (outer * inv[...]).astype(BF)
        part = jnp.dot(panel, ta[...], preferred_element_type=F32)
        mapped = part if mapped is None else mapped + part
    prod = mapped * tg_ref[...].astype(F32)
    out_ref[...] += jnp.sum(prod.reshape(prod.shape[0] // 8, 8, prod.shape[1]), axis=0)


def chunk_scores(rg, ra, inv_own, inv_oth, tg_t, ta_own_t, ta_oth_t):
    tokens, rows = rg.shape
    half = inv_own.shape[1]
    train = tg_t.shape[1]
    tile = 256
    return pl.pallas_call(
        panel_kernel,
        out_shape=jax.ShapeDtypeStruct((8, train), F32),
        grid=(rows // tile,),
        in_specs=[
            pl.BlockSpec((tokens, tile), lambda i: (0, i)),
            pl.BlockSpec((tokens, 2 * half), lambda i: (0, 0)),
            pl.BlockSpec((tile, half), lambda i: (i, 0)),
            pl.BlockSpec((tile, half), lambda i: (i, 0)),
            pl.BlockSpec((tile, train), lambda i: (i, 0)),
            pl.BlockSpec((half, train), lambda i: (0, 0)),
            pl.BlockSpec((half, train), lambda i: (0, 0)),
        ],
        out_specs=pl.BlockSpec((8, train), lambda i: (0, 0)),
        cost_estimate=pl.CostEstimate(
            flops=2 * rows * 2 * half * (tokens + train),
            bytes_accessed=8 * rows * half,
            transcendentals=0,
        ),
    )(rg, ra, inv_own, inv_oth, tg_t, ta_own_t, ta_oth_t)


def shards(R, C, query_acts, query_grads, act_basis, grad_basis, eigenvalues, train_acts, train_grads):
    n = C // 2
    assert n == R and R & (R - 1) == 0
    r = lax.axis_index("row")
    c = lax.axis_index("col")
    z, p = c // 2, c % 2

    def core(x):
        return lax.ppermute(x, "col", [(k, k ^ 1) for k in range(C)])

    def across(x, d):
        return lax.ppermute(x, "row", [(k, k ^ d) for k in range(R)])

    def along(x, step, senders):
        return lax.ppermute(
            x, "col", [(2 * k + q, 2 * (k + step) + q) for k in senders for q in (0, 1)]
        )

    m = query_acts.shape[0]
    part_tg = train_grads.shape[0]
    part_ta = train_acts.shape[0]
    train = part_tg * C

    packet = jnp.concatenate([query_acts, train_grads], axis=0)
    up, down = {0: packet}, {0: packet}
    for d in range(1, n):
        up[d] = along(up[d - 1], 1, range(d - 1, n - 1))
        down[d] = along(down[d - 1], -1, range(1, n - d + 1))

    halves = query_grads.reshape(2, m, query_grads.shape[1])
    keep = jnp.where(p == 0, halves[0], halves[1])
    send = jnp.where(p == 0, halves[1], halves[0])
    grads_in = {0: [jnp.concatenate([keep, core(send)], axis=1)]}
    for s in range(1, R):
        low, high = s & -s, 1 << (s.bit_length() - 1)
        if low == high:
            grads_in[s] = [across(jnp.concatenate(grads_in[s ^ low], axis=0), low)]
        else:
            first = jnp.concatenate(grads_in[s ^ high], axis=0)[: m // 2]
            second = jnp.concatenate(grads_in[s ^ low], axis=0)[m // 2 :]
            grads_in[s] = [across(first, high), across(second, low)]

    acts_rot = jnp.concatenate([act_basis, core(act_basis)], axis=1)
    grads_rot = jnp.concatenate([grad_basis, core(grad_basis)], axis=0)
    inv_own = 1.0 / (QUERY_LEN * (eigenvalues + damping))
    inv_oth = core(inv_own)

    parts = [
        jnp.concatenate(
            [jnp.dot(x, grads_rot, preferred_element_type=F32).astype(BF) for x in grads_in[s]], axis=0
        )
        for s in range(R)
    ]

    rounds = R + n - 2
    got_up, got_down = {}, {}
    for t in range(rounds):
        ups = [min(max(t - k, 0), R - 1) for k in range(n)]
        downs = [min(max(t - (n - 1 - k), 0), R - 1) for k in range(n)]
        mine_up = choose(z, [parts[s] for s in ups])
        mine_down = choose(z, [parts[s] for s in downs])
        if t > 0:
            mine_up = (mine_up.astype(F32) + got_up[t - 1].astype(F32)).astype(BF)
            mine_down = (mine_down.astype(F32) + got_down[t - 1].astype(F32)).astype(BF)
        got_up[t] = along(mine_up, 1, [k for k in range(n - 1) if 0 <= t - k < R])
        got_down[t] = along(mine_down, -1, [k for k in range(1, n) if 0 <= t - (n - 1 - k) < R])

    order = []
    for k in range(n):
        mine = [(0, 0, k)]
        for d in range(1, n):
            if k - d >= 0:
                mine.append((1, d, k - d))
            if k + d < n:
                mine.append((-1, d, k + d))
        order.append(mine)
    bits = [1 << b for b in range(R.bit_length() - 1)]
    rotated = []
    for a in range(n):
        buffers = [(up if order[k][a][0] >= 0 else down)[order[k][a][1]] for k in range(n)]
        x = choose(z, buffers)[:m]
        v = jnp.dot(x, acts_rot, preferred_element_type=F32).astype(BF)
        turn = a % len(bits)
        for b in bits[turn:] + bits[:turn]:
            v = (v.astype(F32) + across(v, b).astype(F32)).astype(BF)
        rotated.append(v)

    tg_mine = []
    for k in range(n):
        tg_mine.append(choose(z, [(up[j - k] if j >= k else down[k - j]) for j in range(n)])[m:])
    tg_mine = jnp.stack(tg_mine)
    tg_oth = core(tg_mine)
    tg = jnp.stack([jnp.where(p == 0, tg_mine, tg_oth), jnp.where(p == 0, tg_oth, tg_mine)], axis=1)
    tg_t = tg.reshape(train, tg.shape[-1]).T
    ta_slots = {0: train_acts}
    for s in range(1, R):
        high = 1 << (s.bit_length() - 1)
        ta_slots[s] = across(ta_slots[s ^ high], high)
    ta = jnp.concatenate([choose(r, [ta_slots[b ^ k] for k in range(R)]) for b in range(R)], axis=0)
    ta_own_t = ta.T
    ta_oth_t = core(ta_own_t)

    slot_scores = []
    zero = jnp.zeros_like(parts[0])
    for s in range(R):
        below = choose(z, [zero] + [got_up[s + k - 1] for k in range(1, n)])
        above = choose(z, [got_down[s + n - 2 - k] for k in range(n - 1)] + [zero])
        rg = (parts[s].astype(F32) + below.astype(F32) + above.astype(F32)).astype(BF)
        place = [[None] * R for _ in range(n)]
        for k in range(n):
            for a in range(n):
                place[k][order[k][a][2]] = a
        table = jnp.array(place, jnp.int32)
        at = table[z, r ^ s]
        ra = choose(at, rotated)
        slot_scores.append(
            chunk_scores(rg, ra, inv_own, inv_oth, tg_t, ta_own_t, ta_oth_t).sum(0)
        )
    by_slot = jnp.stack(slot_scores)
    by_chunk = jnp.stack([choose(r, [by_slot[k ^ j] for j in range(R)]) for k in range(n)])
    other = core(by_chunk)
    chunks = jnp.stack([jnp.where(p == 0, by_chunk, other), jnp.where(p == 0, other, by_chunk)], axis=1)
    queries = C * m // QUERY_LEN
    value = chunks.reshape(queries, 2 * n // queries, train).sum(1) / D
    blocks = value.reshape(queries, R * C, train // (R * C)).transpose(1, 0, 2)
    keep_half = jnp.where(jnp.arange(R * C) % 2 == p, 1.0, 0.0)[:, None, None]
    got = lax.all_to_all(blocks * keep_half, ("row", "col"), 0, 0, tiled=True)
    return got.sum(0)


def solution(mesh):
    R, C = mesh.shape["row"], mesh.shape["col"]

    def body(*arrays):
        return shards(R, C, *arrays)

    return jax.shard_map(
        body,
        mesh=mesh,
        in_specs=(
            P("col", "row"),
            P("row", "col"),
            P("row", "col"),
            P("col", "row"),
            P("row", "col"),
            P("row", "col"),
            P("col", "row"),
        ),
        out_specs=P(None, ("row", "col")),
        check_vma=False,
    )
```

```python
import functools
import math

import jax
import jax.numpy as jnp
from jax import lax
from jax.experimental import pallas as pl
from jax.experimental.pallas import tpu as pltpu
from jax.sharding import PartitionSpec as P


D = 6144
QUERY_LEN = 256
damping = 0.01


BF = jnp.bfloat16
F32 = jnp.float32


def choose(index, options):
    out = options[-1]
    for k in range(len(options) - 2, -1, -1):
        if options[k] is not out:
            out = jnp.where(index == k, options[k], out)
    return out


def after(x, *tokens):
    return lax.optimization_barrier((x,) + tokens)[0]


def panel_kernel(
    tables,
    pick_ref,
    part_ref,
    *refs,
):
    below_pick, above_pick, n_ups, n_downs, n_acts = tables
    ups, refs = refs[:n_ups], refs[n_ups:]
    downs, refs = refs[:n_downs], refs[n_downs:]
    acts, refs = refs[:n_acts], refs[n_acts:]
    adds, refs = refs[:n_acts], refs[n_acts:]
    inv_own, inv_oth, tg_ref, ta_own, ta_oth, out_ref = refs[:6]
    buf, acts_buf, acc, sems = refs[6:]
    step = pl.program_id(0)

    @pl.when(step == 0)
    def _():
        acc[...] = jnp.zeros_like(acc)
        z, at = pick_ref[0], pick_ref[1]
        own = pltpu.make_async_copy(part_ref, buf.at[0], sems.at[0])
        own.start()
        for k in range(len(below_pick)):
            for slot, picks, sources in ((1, below_pick, ups), (2, above_pick, downs)):
                if picks[k] is not None:

                    @pl.when(z == k)
                    def _(src=sources[picks[k]], slot=slot):
                        pltpu.make_async_copy(src, buf.at[slot], sems.at[slot]).start()
                else:

                    @pl.when(z == k)
                    def _(slot=slot):
                        pltpu.make_async_copy(part_ref, buf.at[slot], sems.at[slot]).start()

        for k in range(n_acts):

            @pl.when(at == k)
            def _(src=acts[k]):
                pltpu.make_async_copy(src, acts_buf.at[0], sems.at[3]).start()

            @pl.when(at == k)
            def _(src=adds[k]):
                pltpu.make_async_copy(src, acts_buf.at[1], sems.at[4]).start()

        own.wait()
        pltpu.make_async_copy(part_ref, buf.at[1], sems.at[1]).wait()
        pltpu.make_async_copy(part_ref, buf.at[2], sems.at[2]).wait()
        no_below = [k for k in range(len(below_pick)) if below_pick[k] is None]
        no_above = [k for k in range(len(above_pick)) if above_pick[k] is None]
        total = buf[0].astype(F32)
        for slot, absent in ((1, no_below), (2, no_above)):
            keep = functools.reduce(jnp.logical_and, [z != k for k in absent])
            total = total + jnp.where(keep, buf[slot].astype(F32), 0.0)
        buf[0] = total.astype(BF)
        pltpu.make_async_copy(acts[0], acts_buf.at[0], sems.at[3]).wait()
        pltpu.make_async_copy(acts[0], acts_buf.at[1], sems.at[4]).wait()
        acts_buf[0] = (acts_buf[0].astype(F32) + acts_buf[1].astype(F32)).astype(BF)

    cols = inv_own.shape[1]
    half = acts_buf.shape[2] // 2
    total = None
    for first, inv, ta in ((0, inv_own, ta_own), (half, inv_oth, ta_oth)):
        at_col = pl.multiple_of(first + step * cols, 128)
        outer = lax.dot_general(
            buf[0],
            acts_buf[0, :, pl.ds(at_col, cols)],
            (((0,), (0,)), ((), ())),
            preferred_element_type=F32,
        )
        panel = (outer * inv[...]).astype(BF)
        mapped = jnp.dot(tg_ref[...], panel, preferred_element_type=F32)
        prod = mapped * ta[...].astype(F32)
        for q in range(cols // 128):
            piece = prod[:, q * 128 : (q + 1) * 128]
            total = piece if total is None else total + piece
    acc[...] += total

    @pl.when(step == pl.num_programs(0) - 1)
    def _():
        out_ref[...] = lax.dot_general(
            jnp.ones((8, 128), F32),
            acc[...],
            (((1,), (1,)), ((), ())),
            precision=lax.Precision.HIGHEST,
            preferred_element_type=F32,
        )


def chunk_scores(pick, tables, part, ups, downs, acts, adds, inv_own, inv_oth, tg, ta_own, ta_oth):
    rows, half = inv_own.shape
    train = tg.shape[0]
    cols = math.gcd(half, 256)
    anywhere = pl.BlockSpec(memory_space=pl.ANY)
    below_pick, above_pick = tables
    return pl.pallas_call(
        functools.partial(
            panel_kernel, (below_pick, above_pick, len(ups), len(downs), len(acts))
        ),
        out_shape=jax.ShapeDtypeStruct((8, train), F32),
        grid_spec=pltpu.PrefetchScalarGridSpec(
            num_scalar_prefetch=1,
            grid=(half // cols,),
            in_specs=[anywhere] * (1 + len(ups) + len(downs) + 2 * len(acts))
            + [
                pl.BlockSpec((rows, cols), lambda j, _: (0, j)),
                pl.BlockSpec((rows, cols), lambda j, _: (0, j)),
                pl.BlockSpec((train, rows), lambda j, _: (0, 0)),
                pl.BlockSpec((train, cols), lambda j, _: (0, j)),
                pl.BlockSpec((train, cols), lambda j, _: (0, j)),
            ],
            out_specs=pl.BlockSpec((8, train), lambda j, _: (0, 0)),
            scratch_shapes=[
                pltpu.VMEM((3,) + part.shape, BF),
                pltpu.VMEM((2,) + acts[0].shape, BF),
                pltpu.VMEM((train, 128), F32),
                pltpu.SemaphoreType.DMA((5,)),
            ],
        ),
        compiler_params=pltpu.CompilerParams(vmem_limit_bytes=24 << 20),
        cost_estimate=pl.CostEstimate(
            flops=4 * rows * half * (part.shape[0] + train),
            bytes_accessed=8 * rows * half,
            transcendentals=0,
        ),
    )(pick, part, *ups, *downs, *acts, *adds, inv_own, inv_oth, tg, ta_own, ta_oth)


def shards(R, C, query_acts, query_grads, act_basis, grad_basis, eigenvalues, train_acts, train_grads):
    n = C // 2
    assert n == R and R & (R - 1) == 0
    r = lax.axis_index("row")
    c = lax.axis_index("col")
    z, p = c // 2, c % 2

    def core(x):
        return lax.ppermute(x, "col", [(k, k ^ 1) for k in range(C)])

    def across(x, d):
        return lax.ppermute(x, "row", [(k, k ^ d) for k in range(R)])

    def along(x, step, senders):
        pairs = [(2 * k + q, 2 * (k + step) + q) for k in senders for q in (0, 1)]
        return lax.ppermute(x, "col", pairs)

    m = query_acts.shape[0]
    part_tg = train_grads.shape[0]
    part_ta = train_acts.shape[0]
    train = part_tg * C

    packet = jnp.concatenate([query_acts, train_grads], axis=0)
    up, down = {0: packet}, {0: packet}
    for d in range(1, n):
        up[d] = along(up[d - 1], 1, range(d - 1, n - 1))
        down[d] = along(down[d - 1], -1, range(1, n - d + 1))

    halves = query_grads.reshape(2, m, query_grads.shape[1])
    keep = jnp.where(p == 0, halves[0], halves[1])
    send = jnp.where(p == 0, halves[1], halves[0])
    half_ta = part_ta // 2
    side = jnp.concatenate([train_acts[:half_ta], train_acts[half_ta:]], axis=1)
    mine = jnp.concatenate([keep, core(send)], axis=1)
    mine = jnp.concatenate([mine, side], axis=0)
    height = mine.shape[0]
    split = height // 16 * 8
    grads_in = {0: mine}
    bits = [1 << b for b in range(R.bit_length() - 1)]
    for bit in bits:
        grads_in[bit] = across(mine, bit)

    acts_rot = jnp.concatenate([act_basis, core(act_basis)], axis=1)
    grads_rot = jnp.concatenate([grad_basis, core(grad_basis)], axis=0)
    inv_own = 1.0 / (QUERY_LEN * (eigenvalues + damping))
    inv_oth = core(inv_own)

    def part_of(s):
        return jnp.dot(grads_in[s][:m], grads_rot, preferred_element_type=F32).astype(BF)

    order = []
    for k in range(n):
        mine = [(0, 0, k)]
        for d in range(1, n):
            if k - d >= 0:
                mine.append((1, d, k - d))
            if k + d < n:
                mine.append((-1, d, k + d))
        order.append(mine)

    def acts_of(a):
        buffers = [(up if order[k][a][0] >= 0 else down)[order[k][a][1]] for k in range(n)]
        x = choose(z, buffers)[:m]
        return jnp.dot(x, acts_rot, preferred_element_type=F32).astype(BF)

    parts = {0: part_of(0)}
    first_acts = {0: acts_of(0), 1: acts_of(1)}
    for level in range(2, len(bits) + 1):
        for s in range(1, R):
            if bin(s).count("1") != level:
                continue
            low, high = s & -s, 1 << (s.bit_length() - 1)
            one, two = [
                jnp.concatenate(x, axis=0) if isinstance(x, tuple) else x
                for x in (grads_in[s ^ high], grads_in[s ^ low])
            ]
            if level == 2:
                one, two = after(one, first_acts[1], parts[0]), after(two, first_acts[1], parts[0])
            first = across(one[:split], high)
            second = across(two[split:], low)
            grads_in[s] = (first, second)
    acts, adds = [], []
    for a in range(n):
        v = first_acts[a] if a in first_acts else acts_of(a)
        turn = a % len(bits)
        turns = bits[turn:] + bits[:turn]
        for i, b in enumerate(turns):
            got = across(v, b)
            if i < len(bits) - 1:
                v = (v.astype(F32) + got.astype(F32)).astype(BF)
        acts.append(v)
        adds.append(got)

    rounds = R + n - 2
    got_up, got_down, sent = {}, {}, {}
    for t in range(rounds):
        if t not in parts and t < R:
            if t & (t - 1):
                pieces = [after(x, sent[t - 1]) for x in grads_in[t]]
                grads_in[t] = jnp.concatenate(pieces, axis=0)
            parts[t] = part_of(t)
        ups = [min(max(t - k, 0), R - 1) for k in range(n)]
        downs = [min(max(t - (n - 1 - k), 0), R - 1) for k in range(n)]
        mine_up = choose(z, [parts[s] for s in ups])
        mine_down = choose(z, [parts[s] for s in downs])
        if t > 0:
            mine_up = (mine_up.astype(F32) + got_up[t - 1].astype(F32)).astype(BF)
            mine_down = (mine_down.astype(F32) + got_down[t - 1].astype(F32)).astype(BF)
        sent[t] = mine_up
        got_up[t] = along(mine_up, 1, [k for k in range(n - 1) if 0 <= t - k < R])
        got_down[t] = along(mine_down, -1, [k for k in range(1, n) if 0 <= t - (n - 1 - k) < R])

    token = sent[n - 1]
    up = {k: after(up[k], token) for k in up}
    down = {k: after(down[k], token) for k in down if k > 0}
    tg_mine = []
    for k in range(n):
        tg_mine.append(choose(z, [(up[j - k] if j >= k else down[k - j]) for j in range(n)])[m:])
    tg_mine = jnp.stack(tg_mine)
    tg_oth = core(tg_mine)
    tg = jnp.stack([jnp.where(p == 0, tg_mine, tg_oth), jnp.where(p == 0, tg_oth, tg_mine)], axis=1)
    tg = tg.reshape(train, tg.shape[-1])
    width = train_acts.shape[1]
    sides = [after(grads_in[k], token)[m:] for k in range(R)]
    ta = []
    for b in range(R):
        side = choose(r, [sides[b ^ k] for k in range(R)])
        ta.extend([side[:, :width], side[:, width:]])
    ta_own = jnp.concatenate(ta, axis=0)
    ta_oth = core(ta_own)

    slot_scores = []
    for s in range(R):
        place = [[None] * n for _ in range(n)]
        for k in range(n):
            for a in range(n):
                place[k][order[k][a][2]] = jnp.int32(a)
        at = choose(z, [choose(r, [place[k][j ^ s] for j in range(R)]) for k in range(n)])
        below = [None] + list(range(n - 1))
        above = list(range(n - 2, -1, -1)) + [None]
        out = chunk_scores(
            jnp.stack([z, at]).astype(jnp.int32),
            (below, above),
            parts[s],
            [got_up[s + k] for k in range(n - 1)],
            [got_down[s + k] for k in range(n - 1)],
            acts,
            adds,
            inv_own,
            inv_oth,
            tg,
            ta_own,
            ta_oth,
        )
        slot_scores.append(out[0])
    by_slot = jnp.stack(slot_scores)
    by_chunk = jnp.stack([choose(r, [by_slot[k ^ j] for j in range(R)]) for k in range(n)])
    other = core(by_chunk)
    chunks = jnp.stack([jnp.where(p == 0, by_chunk, other), jnp.where(p == 0, other, by_chunk)], axis=1)
    queries = C * m // QUERY_LEN
    value = chunks.reshape(queries, 2 * n // queries, train).sum(1) / D
    blocks = value.reshape(queries, R * C, train // (R * C)).transpose(1, 0, 2)
    keep_half = jnp.where(jnp.arange(R * C) % 2 == p, 1.0, 0.0)[:, None, None]
    got = lax.all_to_all(blocks * keep_half, ("row", "col"), 0, 0, tiled=True)
    return got.sum(0)


def solution(mesh):
    R, C = mesh.shape["row"], mesh.shape["col"]

    def body(*arrays):
        return shards(R, C, *arrays)

    return jax.shard_map(
        body,
        mesh=mesh,
        in_specs=(
            P("col", "row"),
            P("row", "col"),
            P("row", "col"),
            P("col", "row"),
            P("row", "col"),
            P("row", "col"),
            P("col", "row"),
        ),
        out_specs=P(None, ("row", "col")),
        check_vma=False,
    )
```

```python
import functools
import math

import jax
import jax.numpy as jnp
from jax import lax
from jax.experimental import pallas as pl
from jax.experimental.pallas import tpu as pltpu
from jax.sharding import PartitionSpec as P


D = 6144
QUERY_LEN = 256
damping = 0.01


BF = jnp.bfloat16
F32 = jnp.float32


def choose(index, options):
    out = options[-1]
    for k in range(len(options) - 2, -1, -1):
        if options[k] is not out:
            out = jnp.where(index == k, options[k], out)
    return out


def after(x, *tokens):
    return lax.optimization_barrier((x,) + tokens)[0]


def panel_kernel(
    tables,
    pick_ref,
    part_ref,
    *refs,
):
    below_pick, above_pick, chunk, up_pieces, down_pieces, n_acts = tables
    ups, downs = [], []
    for counts, into in ((up_pieces, ups), (down_pieces, downs)):
        for count in counts:
            into.append(refs[:count])
            refs = refs[count:]
    acts, refs = refs[:n_acts], refs[n_acts:]
    adds, refs = refs[:n_acts], refs[n_acts:]
    inv_own, inv_oth, tg_ref, ta_own, ta_oth, out_ref = refs[:6]
    buf, acts_buf, acc, sems = refs[6:]
    step = pl.program_id(0)

    @pl.when(step == 0)
    def _():
        acc[...] = jnp.zeros_like(acc)
        z, at = pick_ref[0], pick_ref[1 + chunk]
        own = pltpu.make_async_copy(part_ref, buf.at[0], sems.at[0])
        own.start()
        mid = part_ref.shape[0] // 2
        halves = (pl.ds(0, mid), pl.ds(mid, mid))

        def copy(pieces, slot, h):
            src = pieces[h] if len(pieces) > 1 else pieces[0].at[halves[h]]
            return pltpu.make_async_copy(src, buf.at[slot, halves[h]], sems.at[1 + 2 * (slot - 1) + h])

        for k in range(len(below_pick)):
            for slot, picks, sources in ((1, below_pick, ups), (2, above_pick, downs)):
                pieces = (part_ref,) if picks[k] is None else sources[picks[k]]

                @pl.when(z == k)
                def _(pieces=pieces, slot=slot):
                    copy(pieces, slot, 0).start()
                    copy(pieces, slot, 1).start()

        for k in range(n_acts):

            @pl.when(at == k)
            def _(src=acts[k]):
                pltpu.make_async_copy(src, acts_buf.at[0], sems.at[5]).start()

            @pl.when(at == k)
            def _(src=adds[k]):
                pltpu.make_async_copy(src, acts_buf.at[1], sems.at[6]).start()

        own.wait()
        for slot in (1, 2):
            for h in (0, 1):
                copy((part_ref,), slot, h).wait()
        no_below = [k for k in range(len(below_pick)) if below_pick[k] is None]
        no_above = [k for k in range(len(above_pick)) if above_pick[k] is None]
        total = buf[0].astype(F32)
        for slot, absent in ((1, no_below), (2, no_above)):
            keep = functools.reduce(jnp.logical_and, [z != k for k in absent])
            total = total + jnp.where(keep, buf[slot].astype(F32), 0.0)
        buf[0] = total.astype(BF)
        pltpu.make_async_copy(acts[0], acts_buf.at[0], sems.at[5]).wait()
        pltpu.make_async_copy(acts[0], acts_buf.at[1], sems.at[6]).wait()
        acts_buf[0] = (acts_buf[0].astype(F32) + acts_buf[1].astype(F32)).astype(BF)

    cols = inv_own.shape[1]
    half = acts_buf.shape[2] // 2
    total = None
    for first, inv, ta in ((0, inv_own, ta_own), (half, inv_oth, ta_oth)):
        at_col = pl.multiple_of(first + step * cols, 128)
        outer = lax.dot_general(
            buf[0],
            acts_buf[0, :, pl.ds(at_col, cols)],
            (((0,), (0,)), ((), ())),
            preferred_element_type=F32,
        )
        panel = (outer * inv[...]).astype(BF)
        mapped = jnp.dot(tg_ref[...], panel, preferred_element_type=F32)
        prod = mapped * ta[...].astype(F32)
        for q in range(cols // 128):
            piece = prod[:, q * 128 : (q + 1) * 128]
            total = piece if total is None else total + piece
    acc[...] += total

    @pl.when(step == pl.num_programs(0) - 1)
    def _():
        out_ref[...] = lax.dot_general(
            jnp.ones((8, 128), F32),
            acc[...],
            (((1,), (1,)), ((), ())),
            precision=lax.Precision.HIGHEST,
            preferred_element_type=F32,
        )


def chunk_scores(pick, tables, part, ups, downs, acts, adds, inv_own, inv_oth, tg, ta_own, ta_oth):
    rows, half = inv_own.shape
    train = tg.shape[0]
    cols = math.gcd(half, 256)
    anywhere = pl.BlockSpec(memory_space=pl.ANY)
    below_pick, above_pick, chunk = tables
    flat = [x for pieces in (*ups, *downs) for x in pieces]
    return pl.pallas_call(
        functools.partial(
            panel_kernel,
            (below_pick, above_pick, chunk, [len(x) for x in ups], [len(x) for x in downs], len(acts)),
        ),
        out_shape=jax.ShapeDtypeStruct((8, train), F32),
        grid_spec=pltpu.PrefetchScalarGridSpec(
            num_scalar_prefetch=1,
            grid=(half // cols,),
            in_specs=[anywhere] * (1 + len(flat) + 2 * len(acts))
            + [
                pl.BlockSpec((rows, cols), lambda j, _: (0, j)),
                pl.BlockSpec((rows, cols), lambda j, _: (0, j)),
                pl.BlockSpec((train, rows), lambda j, _: (0, 0)),
                pl.BlockSpec((train, cols), lambda j, _: (0, j)),
                pl.BlockSpec((train, cols), lambda j, _: (0, j)),
            ],
            out_specs=pl.BlockSpec((8, train), lambda j, _: (0, 0)),
            scratch_shapes=[
                pltpu.VMEM((3,) + part.shape, BF),
                pltpu.VMEM((2,) + acts[0].shape, BF),
                pltpu.VMEM((train, 128), F32),
                pltpu.SemaphoreType.DMA((7,)),
            ],
        ),
        compiler_params=pltpu.CompilerParams(vmem_limit_bytes=24 << 20),
        cost_estimate=pl.CostEstimate(
            flops=4 * rows * half * (part.shape[0] + train),
            bytes_accessed=8 * rows * half,
            transcendentals=0,
        ),
    )(pick, part, *flat, *acts, *adds, inv_own, inv_oth, tg, ta_own, ta_oth)


def shards(R, C, query_acts, query_grads, act_basis, grad_basis, eigenvalues, train_acts, train_grads):
    n = C // 2
    assert n == R and R & (R - 1) == 0
    r = lax.axis_index("row")
    c = lax.axis_index("col")
    z, p = c // 2, c % 2

    def core(x):
        return lax.ppermute(x, "col", [(k, k ^ 1) for k in range(C)])

    def across(x, d):
        return lax.ppermute(x, "row", [(k, k ^ d) for k in range(R)])

    def along(x, step, senders):
        pairs = [(2 * k + q, 2 * (k + step) + q) for k in senders for q in (0, 1)]
        return lax.ppermute(x, "col", pairs)

    m = query_acts.shape[0]
    part_tg = train_grads.shape[0]
    part_ta = train_acts.shape[0]
    train = part_tg * C

    up, down = {0: query_acts}, {0: query_acts}
    tg_up, tg_down = {0: train_grads}, {0: train_grads}
    for d in range(1, n):
        going_up, going_down = range(d - 1, n - 1), range(1, n - d + 1)
        up[d] = along(up[d - 1], 1, going_up)
        down[d] = along(down[d - 1], -1, going_down)
        tg_up[d] = along(tg_up[d - 1], 1, going_up)
        tg_down[d] = along(tg_down[d - 1], -1, going_down)

    halves = query_grads.reshape(2, m, query_grads.shape[1])
    keep = jnp.where(p == 0, halves[0], halves[1])
    send = jnp.where(p == 0, halves[1], halves[0])
    half_ta = part_ta // 2
    side = jnp.concatenate([train_acts[:half_ta], train_acts[half_ta:]], axis=1)
    mine = jnp.concatenate([keep, core(send)], axis=1)
    mine = jnp.concatenate([mine, side], axis=0)
    height = mine.shape[0]
    split = height // 16 * 8
    grads_in = {0: mine}
    bits = [1 << b for b in range(R.bit_length() - 1)]
    for bit in bits:
        grads_in[bit] = across(mine, bit)

    acts_rot = jnp.concatenate([act_basis, core(act_basis)], axis=1)
    grads_rot = jnp.concatenate([grad_basis, core(grad_basis)], axis=0)
    inv_own = 1.0 / (QUERY_LEN * (eigenvalues + damping))
    inv_oth = core(inv_own)

    def part_of(s):
        return jnp.dot(grads_in[s][:m], grads_rot, preferred_element_type=F32).astype(BF)

    order = []
    for k in range(n):
        mine = [(0, 0, k)]
        for d in range(1, n):
            if k - d >= 0:
                mine.append((1, d, k - d))
            if k + d < n:
                mine.append((-1, d, k + d))
        order.append(mine)

    def acts_of(a):
        buffers = [(up if order[k][a][0] >= 0 else down)[order[k][a][1]] for k in range(n)]
        x = choose(z, buffers)
        return jnp.dot(x, acts_rot, preferred_element_type=F32).astype(BF)

    parts = {0: part_of(0)}
    first_acts = {0: acts_of(0), 1: acts_of(1)}
    for level in range(2, len(bits) + 1):
        for s in range(1, R):
            if bin(s).count("1") != level:
                continue
            low, high = s & -s, 1 << (s.bit_length() - 1)
            one, two = [
                jnp.concatenate(x, axis=0) if isinstance(x, tuple) else x
                for x in (grads_in[s ^ high], grads_in[s ^ low])
            ]
            if level == 2:
                one, two = after(one, first_acts[1], parts[0]), after(two, first_acts[1], parts[0])
            one, two = one[:split], two[split:]
            first = across(one, high)
            second = across(two, low)
            grads_in[s] = (first, second)
    acts, adds = [], []
    for a in range(n):
        v = first_acts[a] if a in first_acts else acts_of(a)
        turn = a % len(bits)
        turns = bits[turn:] + bits[:turn]
        for i, b in enumerate(turns):
            got = across(v, b)
            if i < len(bits) - 1:
                v = (v.astype(F32) + got.astype(F32)).astype(BF)
        acts.append(v)
        adds.append(got)

    rounds = R + n - 2
    got_up, got_down, sent, sent_down = {}, {}, {}, {}

    def running_sums(t, *gates):
        if t not in parts and t < R:
            if t & (t - 1):
                pieces = [after(x, sent[t - 1]) for x in grads_in[t]]
                grads_in[t] = jnp.concatenate(pieces, axis=0)
            parts[t] = part_of(t)
        ups = [min(max(t - k, 0), R - 1) for k in range(n)]
        downs = [min(max(t - (n - 1 - k), 0), R - 1) for k in range(n)]
        senders_up = [k for k in range(n - 1) if 0 <= t - k < R]
        senders_down = [k for k in range(1, n) if 0 <= t - (n - 1 - k) < R]
        spans = [slice(0, m)] if t == 0 else [slice(0, m // 2), slice(m // 2, m)]
        got_up[t], got_down[t] = [], []
        for h, rows in enumerate(spans):
            if t == 0:
                mine_up = mine_down = parts[0]
            else:
                if t > 1:
                    mine = [got_up[t - 1][h], got_down[t - 1][h]]
                else:
                    mine = [got_up[0][0], got_down[0][0]]
                used = sorted(set(ups + downs))
                tokens = gates if h == 0 else ()
                tokens += (sent[t - 1], sent_down[t - 1]) if h == 0 else (sent[t], sent_down[t])
                from_up, from_down, *now = lax.optimization_barrier(
                    (*mine, *[parts[s] for s in used], *tokens)
                )
                if t == 1:
                    from_up, from_down = from_up[rows], from_down[rows]
                now = dict(zip(used, now))
                mine_up = choose(z, [now[s] for s in ups])[rows].astype(F32)
                mine_down = choose(z, [now[s] for s in downs])[rows].astype(F32)
                mine_up = (mine_up + from_up.astype(F32)).astype(BF)
                mine_down = (mine_down + from_down.astype(F32)).astype(BF)
            if h == 0:
                sent[t], sent_down[t] = mine_up, mine_down
            got_up[t].append(along(mine_up, 1, senders_up))
            got_down[t].append(along(mine_down, -1, senders_down))

    for t in range(n + 1):
        running_sums(t)

    token = sent[n - 1]
    tg_up = {k: after(tg_up[k], token) for k in tg_up}
    tg_down = {k: after(tg_down[k], token) for k in tg_down if k > 0}
    tg_mine = []
    for k in range(n):
        options = [(tg_up[j - k] if j >= k else tg_down[k - j]) for j in range(n)]
        tg_mine.append(choose(z, options))
    tg_mine = jnp.stack(tg_mine)
    tg_oth = core(tg_mine)
    tg = jnp.stack([jnp.where(p == 0, tg_mine, tg_oth), jnp.where(p == 0, tg_oth, tg_mine)], axis=1)
    tg = tg.reshape(train, tg.shape[-1])
    width = train_acts.shape[1]
    sides = [after(grads_in[k], token)[m:] for k in range(R)]
    ta = []
    for b in range(R):
        side = choose(r, [sides[b ^ k] for k in range(R)])
        ta.extend([side[:, :width], side[:, width:]])
    ta_own = jnp.concatenate(ta, axis=0)
    ta_oth = core(ta_own)

    place = [[None] * n for _ in range(n)]
    for k in range(n):
        for a in range(n):
            place[k][order[k][a][2]] = jnp.int32(a)
    pick = [z.astype(jnp.int32)]
    for s in range(R):
        pick.append(choose(z, [choose(r, [place[k][j ^ s] for j in range(R)]) for k in range(n)]))
    pick = jnp.stack(pick)

    def scores_of(s):
        below = [None] + list(range(n - 1))
        above = list(range(n - 2, -1, -1)) + [None]
        out = chunk_scores(
            pick,
            (below, above, s),
            parts[s],
            [got_up[s + k] for k in range(n - 1)],
            [got_down[s + k] for k in range(n - 1)],
            acts,
            adds,
            inv_own,
            inv_oth,
            tg,
            ta_own,
            ta_oth,
        )
        return out

    outs = []
    for t in range(n + 1, rounds):
        outs.append(scores_of(t - n - 1))
        running_sums(t, outs[-1])
    for s in range(len(outs), R):
        outs.append(scores_of(s))
    slot_scores = [out[0] for out in outs]
    by_slot = jnp.stack(slot_scores)
    by_chunk = jnp.stack([choose(r, [by_slot[k ^ j] for j in range(R)]) for k in range(n)])
    share = train // (R * C)
    blocks = (by_chunk / D).reshape(n, R * C, share).transpose(1, 0, 2)
    got = lax.all_to_all(blocks, ("row", "col"), 0, 0, tiled=True)
    value = got.reshape(R * n, 2, n, share).sum(0).transpose(1, 0, 2)
    queries = C * m // QUERY_LEN
    return value.reshape(queries, 2 * n // queries, share).sum(1)


def solution(mesh):
    R, C = mesh.shape["row"], mesh.shape["col"]

    def body(*arrays):
        return shards(R, C, *arrays)

    return jax.shard_map(
        body,
        mesh=mesh,
        in_specs=(
            P("col", "row"),
            P("row", "col"),
            P("row", "col"),
            P("col", "row"),
            P("row", "col"),
            P("row", "col"),
            P("col", "row"),
        ),
        out_specs=P(None, ("row", "col")),
        check_vma=False,
    )
```

```python
import functools
import math

import jax
import jax.numpy as jnp
from jax import lax
from jax.experimental import pallas as pl
from jax.experimental.pallas import tpu as pltpu
from jax.sharding import PartitionSpec as P


D = 6144
QUERY_LEN = 256
damping = 0.01


BF = jnp.bfloat16
F32 = jnp.float32


def choose(index, options):
    out = options[-1]
    for k in range(len(options) - 2, -1, -1):
        if options[k] is not out:
            out = jnp.where(index == k, options[k], out)
    return out


def after(x, *tokens):
    return lax.optimization_barrier((x,) + tokens)[0]


def panel_kernel(
    tables,
    pick_ref,
    part_ref,
    *refs,
):
    below_pick, above_pick, chunk, up_pieces, down_pieces, n_acts = tables
    ups, downs = [], []
    for counts, into in ((up_pieces, ups), (down_pieces, downs)):
        for count in counts:
            into.append(refs[:count])
            refs = refs[count:]
    acts, refs = refs[:n_acts], refs[n_acts:]
    adds, refs = refs[:n_acts], refs[n_acts:]
    eig_own, eig_oth, tg_ref, ta_own, ta_oth, out_ref = refs[:6]
    buf, acts_buf, acc, sems = refs[6:]
    step = pl.program_id(0)

    @pl.when(step == 0)
    def _():
        acc[...] = jnp.zeros_like(acc)
        z, at = pick_ref[0], pick_ref[1 + chunk]
        own = pltpu.make_async_copy(part_ref, buf.at[0], sems.at[0])
        own.start()
        mid = part_ref.shape[0] // 2
        halves = (pl.ds(0, mid), pl.ds(mid, mid))

        def copy(pieces, slot, h):
            src = pieces[h] if len(pieces) > 1 else pieces[0].at[halves[h]]
            return pltpu.make_async_copy(src, buf.at[slot, halves[h]], sems.at[1 + 2 * (slot - 1) + h])

        for k in range(len(below_pick)):
            for slot, picks, sources in ((1, below_pick, ups), (2, above_pick, downs)):
                pieces = (part_ref,) if picks[k] is None else sources[picks[k]]

                @pl.when(z == k)
                def _(pieces=pieces, slot=slot):
                    copy(pieces, slot, 0).start()
                    copy(pieces, slot, 1).start()

        for k in range(n_acts):

            @pl.when(at == k)
            def _(src=acts[k]):
                pltpu.make_async_copy(src, acts_buf.at[0], sems.at[5]).start()

            @pl.when(at == k)
            def _(src=adds[k]):
                pltpu.make_async_copy(src, acts_buf.at[1], sems.at[6]).start()

        own.wait()
        for slot in (1, 2):
            for h in (0, 1):
                copy((part_ref,), slot, h).wait()
        no_below = [k for k in range(len(below_pick)) if below_pick[k] is None]
        no_above = [k for k in range(len(above_pick)) if above_pick[k] is None]
        total = buf[0].astype(F32)
        for slot, absent in ((1, no_below), (2, no_above)):
            keep = functools.reduce(jnp.logical_and, [z != k for k in absent])
            total = total + jnp.where(keep, buf[slot].astype(F32), 0.0)
        buf[0] = total.astype(BF)
        pltpu.make_async_copy(acts[0], acts_buf.at[0], sems.at[5]).wait()
        pltpu.make_async_copy(acts[0], acts_buf.at[1], sems.at[6]).wait()
        acts_buf[0] = (acts_buf[0].astype(F32) + acts_buf[1].astype(F32)).astype(BF)

    cols = eig_own.shape[1]
    half = acts_buf.shape[2] // 2
    total = None
    for first, eig, ta in ((0, eig_own, ta_own), (half, eig_oth, ta_oth)):
        at_col = pl.multiple_of(first + step * cols, 128)
        outer = lax.dot_general(
            buf[0],
            acts_buf[0, :, pl.ds(at_col, cols)],
            (((0,), (0,)), ((), ())),
            preferred_element_type=F32,
        )
        panel = (outer / (QUERY_LEN * (eig[...] + damping))).astype(BF)
        mapped = jnp.dot(tg_ref[...], panel, preferred_element_type=F32)
        prod = mapped * ta[...].astype(F32)
        for q in range(cols // 128):
            piece = prod[:, q * 128 : (q + 1) * 128]
            total = piece if total is None else total + piece
    acc[...] += total

    @pl.when(step == pl.num_programs(0) - 1)
    def _():
        out_ref[...] = lax.dot_general(
            jnp.ones((8, 128), F32),
            acc[...],
            (((1,), (1,)), ((), ())),
            precision=lax.Precision.HIGHEST,
            preferred_element_type=F32,
        )


def chunk_scores(pick, tables, part, ups, downs, acts, adds, eig_own, eig_oth, tg, ta_own, ta_oth):
    rows, half = eig_own.shape
    train = tg.shape[0]
    cols = math.gcd(half, 256)
    anywhere = pl.BlockSpec(memory_space=pl.ANY)
    below_pick, above_pick, chunk = tables
    flat = [x for pieces in (*ups, *downs) for x in pieces]
    return pl.pallas_call(
        functools.partial(
            panel_kernel,
            (below_pick, above_pick, chunk, [len(x) for x in ups], [len(x) for x in downs], len(acts)),
        ),
        out_shape=jax.ShapeDtypeStruct((8, train), F32),
        grid_spec=pltpu.PrefetchScalarGridSpec(
            num_scalar_prefetch=1,
            grid=(half // cols,),
            in_specs=[anywhere] * (1 + len(flat) + 2 * len(acts))
            + [
                pl.BlockSpec((rows, cols), lambda j, _: (0, j)),
                pl.BlockSpec((rows, cols), lambda j, _: (0, j)),
                pl.BlockSpec((train, rows), lambda j, _: (0, 0)),
                pl.BlockSpec((train, cols), lambda j, _: (0, j)),
                pl.BlockSpec((train, cols), lambda j, _: (0, j)),
            ],
            out_specs=pl.BlockSpec((8, train), lambda j, _: (0, 0)),
            scratch_shapes=[
                pltpu.VMEM((3,) + part.shape, BF),
                pltpu.VMEM((2,) + acts[0].shape, BF),
                pltpu.VMEM((train, 128), F32),
                pltpu.SemaphoreType.DMA((7,)),
            ],
        ),
        compiler_params=pltpu.CompilerParams(vmem_limit_bytes=24 << 20),
        cost_estimate=pl.CostEstimate(
            flops=4 * rows * half * (part.shape[0] + train),
            bytes_accessed=8 * rows * half,
            transcendentals=0,
        ),
    )(pick, part, *flat, *acts, *adds, eig_own, eig_oth, tg, ta_own, ta_oth)


def shards(R, C, query_acts, query_grads, act_basis, grad_basis, eigenvalues, train_acts, train_grads):
    n = C // 2
    assert n == R and R & (R - 1) == 0
    r = lax.axis_index("row")
    c = lax.axis_index("col")
    z, p = c // 2, c % 2

    def core(x):
        return lax.ppermute(x, "col", [(k, k ^ 1) for k in range(C)])

    def across(x, d):
        return lax.ppermute(x, "row", [(k, k ^ d) for k in range(R)])

    def along(x, step, senders):
        pairs = [(2 * k + q, 2 * (k + step) + q) for k in senders for q in (0, 1)]
        return lax.ppermute(x, "col", pairs)

    m = query_acts.shape[0]
    part_tg = train_grads.shape[0]
    part_ta = train_acts.shape[0]
    train = part_tg * C

    packet = jnp.concatenate([query_acts, train_grads], axis=0)
    up, down = {0: packet}, {0: packet}
    for d in range(1, n):
        up[d] = along(up[d - 1], 1, range(d - 1, n - 1))
        down[d] = along(down[d - 1], -1, range(1, n - d + 1))

    halves = query_grads.reshape(2, m, query_grads.shape[1])
    keep = jnp.where(p == 0, halves[0], halves[1])
    send = jnp.where(p == 0, halves[1], halves[0])
    half_ta = part_ta // 2
    side = jnp.concatenate([train_acts[:half_ta], train_acts[half_ta:]], axis=1)
    mine = jnp.concatenate([keep, core(send)], axis=1)
    mine = jnp.concatenate([mine, side], axis=0)
    height = mine.shape[0]
    split = height // 16 * 8
    grads_in = {0: mine}
    bits = [1 << b for b in range(R.bit_length() - 1)]
    for bit in bits:
        grads_in[bit] = across(mine, bit)

    acts_rot = jnp.concatenate([act_basis, core(act_basis)], axis=1)
    grads_rot = jnp.concatenate([grad_basis, core(grad_basis)], axis=0)
    eig_oth = core(eigenvalues)

    def part_of(s):
        return jnp.dot(grads_in[s][:m], grads_rot, preferred_element_type=F32).astype(BF)

    order = []
    for k in range(n):
        mine = [(0, 0, k)]
        for d in range(1, n):
            if k - d >= 0:
                mine.append((1, d, k - d))
            if k + d < n:
                mine.append((-1, d, k + d))
        order.append(mine)

    def acts_of(a):
        buffers = [(up if order[k][a][0] >= 0 else down)[order[k][a][1]] for k in range(n)]
        x = choose(z, [x[:m] for x in buffers] if a else [query_acts])
        return jnp.dot(x, acts_rot, preferred_element_type=F32).astype(BF)

    parts = {0: part_of(0)}
    first_acts = {0: acts_of(0), 1: acts_of(1)}
    for level in range(2, len(bits) + 1):
        for s in range(1, R):
            if bin(s).count("1") != level:
                continue
            low, high = s & -s, 1 << (s.bit_length() - 1)
            one, two = [
                jnp.concatenate(x, axis=0) if isinstance(x, tuple) else x
                for x in (grads_in[s ^ high], grads_in[s ^ low])
            ]
            if level == 2:
                one, two = after(one, first_acts[1], parts[0]), after(two, first_acts[1], parts[0])
            one, two = one[:split], two[split:]
            first = across(one, high)
            second = across(two, low)
            grads_in[s] = (first, second)
    acts, adds = [], []
    for a in range(n):
        v = first_acts[a] if a in first_acts else acts_of(a)
        turn = a % len(bits)
        turns = bits[turn:] + bits[:turn]
        for i, b in enumerate(turns):
            got = across(v, b)
            if i < len(bits) - 1:
                v = (v.astype(F32) + got.astype(F32)).astype(BF)
        acts.append(v)
        adds.append(got)

    rounds = R + n - 2
    got_up, got_down, sent, sent_down = {}, {}, {}, {}

    def running_sums(t, *gates):
        if t not in parts and t < R:
            if t & (t - 1):
                pieces = [after(x, sent[t - 1]) for x in grads_in[t]]
                grads_in[t] = jnp.concatenate(pieces, axis=0)
            parts[t] = part_of(t)
        ups = [min(max(t - k, 0), R - 1) for k in range(n)]
        downs = [min(max(t - (n - 1 - k), 0), R - 1) for k in range(n)]
        senders_up = [k for k in range(n - 1) if 0 <= t - k < R]
        senders_down = [k for k in range(1, n) if 0 <= t - (n - 1 - k) < R]
        spans = [slice(0, m)] if t < n - 1 else [slice(0, m // 2), slice(m // 2, m)]
        got_up[t], got_down[t] = [], []
        for h, rows in enumerate(spans):
            if t == 0:
                mine_up = mine_down = parts[0]
            else:
                split_here = len(got_up[t - 1]) < len(spans)
                mine = [x[t - 1][0 if split_here else h] for x in (got_up, got_down)]
                used = sorted(set(ups + downs))
                tokens = gates if h == 0 else ()
                tokens += (sent[t - 1], sent_down[t - 1]) if h == 0 else (sent[t], sent_down[t])
                from_up, from_down, *now = lax.optimization_barrier(
                    (*mine, *[parts[s] for s in used], *tokens)
                )
                if split_here:
                    from_up, from_down = from_up[rows], from_down[rows]
                now = dict(zip(used, now))
                mine_up = choose(z, [now[s] for s in ups])[rows].astype(F32)
                mine_down = choose(z, [now[s] for s in downs])[rows].astype(F32)
                mine_up = (mine_up + from_up.astype(F32)).astype(BF)
                mine_down = (mine_down + from_down.astype(F32)).astype(BF)
            if h == 0:
                sent[t], sent_down[t] = mine_up, mine_down
            got_up[t].append(along(mine_up, 1, senders_up))
            got_down[t].append(along(mine_down, -1, senders_down))

    for t in range(n + 1):
        running_sums(t)

    token = sent[n - 1]
    tg_up = {k: after(up[k], token)[m:] if k else train_grads for k in up}
    tg_down = {k: after(down[k], token)[m:] for k in down if k > 0}
    tg_mine = []
    for k in range(n):
        options = [(tg_up[j - k] if j >= k else tg_down[k - j]) for j in range(n)]
        tg_mine.append(choose(z, options))
    tg_mine = jnp.stack(tg_mine)
    tg_oth = core(tg_mine)
    tg = jnp.stack([jnp.where(p == 0, tg_mine, tg_oth), jnp.where(p == 0, tg_oth, tg_mine)], axis=1)
    tg = tg.reshape(train, tg.shape[-1])
    width = train_acts.shape[1]
    sides = [after(grads_in[k], token)[m:] for k in range(R)]
    ta = []
    for b in range(R):
        side = choose(r, [sides[b ^ k] for k in range(R)])
        ta.extend([side[:, :width], side[:, width:]])
    ta_own = jnp.concatenate(ta, axis=0)
    ta_oth = core(ta_own)

    place = [[None] * n for _ in range(n)]
    for k in range(n):
        for a in range(n):
            place[k][order[k][a][2]] = jnp.int32(a)
    pick = [z.astype(jnp.int32)]
    for s in range(R):
        pick.append(choose(z, [choose(r, [place[k][j ^ s] for j in range(R)]) for k in range(n)]))
    pick = jnp.stack(pick)

    def scores_of(s):
        below = [None] + list(range(n - 1))
        above = list(range(n - 2, -1, -1)) + [None]
        out = chunk_scores(
            pick,
            (below, above, s),
            parts[s],
            [got_up[s + k] for k in range(n - 1)],
            [got_down[s + k] for k in range(n - 1)],
            acts,
            adds,
            eigenvalues,
            eig_oth,
            tg,
            ta_own,
            ta_oth,
        )
        return out

    outs = []
    for t in range(n + 1, rounds):
        outs.append(scores_of(t - n - 1))
        running_sums(t, outs[-1])
    for s in range(len(outs), R):
        outs.append(scores_of(s))
    slot_scores = [out[0] for out in outs]
    by_slot = jnp.stack(slot_scores)
    by_chunk = jnp.stack([choose(r, [by_slot[k ^ j] for j in range(R)]) for k in range(n)])
    share = train // (R * C)
    blocks = (by_chunk / D).reshape(n, R * C, share).transpose(1, 0, 2)
    got = lax.all_to_all(blocks, ("row", "col"), 0, 0, tiled=True)
    value = got.reshape(R * n, 2, n, share).sum(0).transpose(1, 0, 2)
    queries = C * m // QUERY_LEN
    return value.reshape(queries, 2 * n // queries, share).sum(1)


def solution(mesh):
    R, C = mesh.shape["row"], mesh.shape["col"]

    def body(*arrays):
        return shards(R, C, *arrays)

    return jax.shard_map(
        body,
        mesh=mesh,
        in_specs=(
            P("col", "row"),
            P("row", "col"),
            P("row", "col"),
            P("col", "row"),
            P("row", "col"),
            P("row", "col"),
            P("col", "row"),
        ),
        out_specs=P(None, ("row", "col")),
        check_vma=False,
    )
```

```python
import functools
import math

import jax
import jax.numpy as jnp
from jax import lax
from jax.experimental import pallas as pl
from jax.experimental.pallas import tpu as pltpu
from jax.sharding import PartitionSpec as P


D = 6144
QUERY_LEN = 256
damping = 0.01


BF = jnp.bfloat16
F32 = jnp.float32


def choose(index, options):
    out = options[-1]
    for k in range(len(options) - 2, -1, -1):
        if options[k] is not out:
            out = jnp.where(index == k, options[k], out)
    return out


def after(x, *tokens):
    return lax.optimization_barrier((x,) + tokens)[0]


def panel_kernel(tables, pick_ref, *refs):
    source_of, chunk, n_acts = tables
    n_grads = max(source_of) + 1
    grads, refs = refs[:n_grads], refs[n_grads:]
    acts, refs = refs[:n_acts], refs[n_acts:]
    adds, refs = refs[:n_acts], refs[n_acts:]
    eig_own, eig_oth, tg_ref, ta_own, ta_oth, out_ref = refs[:6]
    buf, acts_buf, acc, sems = refs[6:]
    step = pl.program_id(0)

    @pl.when(step == 0)
    def _():
        acc[...] = jnp.zeros_like(acc)
        z, at = pick_ref[0], pick_ref[1 + chunk]
        for d in range(n_grads):
            here = functools.reduce(
                jnp.logical_or, [z == k for k in range(len(source_of)) if source_of[k] == d]
            )

            @pl.when(here)
            def _(src=grads[d]):
                pltpu.make_async_copy(src, buf, sems.at[0]).start()

        for k in range(n_acts):

            @pl.when(at == k)
            def _(src=acts[k]):
                pltpu.make_async_copy(src, acts_buf.at[0], sems.at[1]).start()

            @pl.when(at == k)
            def _(src=adds[k]):
                pltpu.make_async_copy(src, acts_buf.at[1], sems.at[2]).start()

        pltpu.make_async_copy(grads[0], buf, sems.at[0]).wait()
        pltpu.make_async_copy(acts[0], acts_buf.at[0], sems.at[1]).wait()
        pltpu.make_async_copy(acts[0], acts_buf.at[1], sems.at[2]).wait()
        acts_buf[0] = (acts_buf[0].astype(F32) + acts_buf[1].astype(F32)).astype(BF)

    cols = eig_own.shape[1]
    half = acts_buf.shape[2] // 2
    total = None
    for first, eig, ta in ((0, eig_own, ta_own), (half, eig_oth, ta_oth)):
        at_col = pl.multiple_of(first + step * cols, 128)
        outer = lax.dot_general(
            buf[...],
            acts_buf[0, :, pl.ds(at_col, cols)],
            (((0,), (0,)), ((), ())),
            preferred_element_type=F32,
        )
        panel = (outer / (QUERY_LEN * (eig[...] + damping))).astype(BF)
        mapped = jnp.dot(tg_ref[...], panel, preferred_element_type=F32)
        prod = mapped * ta[...].astype(F32)
        for q in range(cols // 128):
            piece = prod[:, q * 128 : (q + 1) * 128]
            total = piece if total is None else total + piece
    acc[...] += total

    @pl.when(step == pl.num_programs(0) - 1)
    def _():
        out_ref[...] = lax.dot_general(
            jnp.ones((8, 128), F32),
            acc[...],
            (((1,), (1,)), ((), ())),
            precision=lax.Precision.HIGHEST,
            preferred_element_type=F32,
        )


def chunk_scores(pick, source_of, chunk, grads, acts, adds, eig_own, eig_oth, tg, ta_own, ta_oth):
    rows, half = eig_own.shape
    train = tg.shape[0]
    cols = math.gcd(half, 256)
    anywhere = pl.BlockSpec(memory_space=pl.ANY)
    return pl.pallas_call(
        functools.partial(
            panel_kernel,
            (source_of, chunk, len(acts)),
        ),
        out_shape=jax.ShapeDtypeStruct((8, train), F32),
        grid_spec=pltpu.PrefetchScalarGridSpec(
            num_scalar_prefetch=1,
            grid=(half // cols,),
            in_specs=[anywhere] * (len(grads) + 2 * len(acts))
            + [
                pl.BlockSpec((rows, cols), lambda j, _: (0, j)),
                pl.BlockSpec((rows, cols), lambda j, _: (0, j)),
                pl.BlockSpec((train, rows), lambda j, _: (0, 0)),
                pl.BlockSpec((train, cols), lambda j, _: (0, j)),
                pl.BlockSpec((train, cols), lambda j, _: (0, j)),
            ],
            out_specs=pl.BlockSpec((8, train), lambda j, _: (0, 0)),
            scratch_shapes=[
                pltpu.VMEM(grads[0].shape, BF),
                pltpu.VMEM((2,) + acts[0].shape, BF),
                pltpu.VMEM((train, 128), F32),
                pltpu.SemaphoreType.DMA((3,)),
            ],
        ),
        compiler_params=pltpu.CompilerParams(vmem_limit_bytes=24 << 20),
        cost_estimate=pl.CostEstimate(
            flops=4 * rows * half * (grads[0].shape[0] + train),
            bytes_accessed=8 * rows * half,
            transcendentals=0,
        ),
    )(pick, *grads, *acts, *adds, eig_own, eig_oth, tg, ta_own, ta_oth)


def shards(R, C, query_acts, query_grads, act_basis, grad_basis, eigenvalues, train_acts, train_grads):
    n = C // 2
    assert n == R and R & (R - 1) == 0
    r = lax.axis_index("row")
    c = lax.axis_index("col")
    z, p = c // 2, c % 2

    def core(x):
        return lax.ppermute(x, "col", [(k, k ^ 1) for k in range(C)])

    def across(x, d):
        return lax.ppermute(x, "row", [(k, k ^ d) for k in range(R)])

    def along(x, step, senders):
        pairs = [(2 * k + q, 2 * (k + step) + q) for k in senders for q in (0, 1)]
        return lax.ppermute(x, "col", pairs)

    m = query_acts.shape[0]
    part_tg = train_grads.shape[0]
    part_ta = train_acts.shape[0]
    train = part_tg * C

    up, down = {0: query_acts}, {0: query_acts}
    for d in range(1, n):
        up[d] = along(up[d - 1], 1, range(d - 1, n - 1))
        down[d] = along(down[d - 1], -1, range(1, n - d + 1))

    halves = query_grads.reshape(2, m, query_grads.shape[1])
    keep = jnp.where(p == 0, halves[0], halves[1])
    send = jnp.where(p == 0, halves[1], halves[0])
    half_ta = part_ta // 2
    side = jnp.concatenate([train_acts[:half_ta], train_acts[half_ta:]], axis=1)
    mine = jnp.concatenate([keep, core(send)], axis=1)
    mine = jnp.concatenate([mine, side], axis=0)
    height = mine.shape[0]
    split = height // 16 * 8
    grads_in = {0: mine}
    bits = [1 << b for b in range(R.bit_length() - 1)]
    for bit in bits:
        grads_in[bit] = across(mine, bit)

    acts_rot = jnp.concatenate([act_basis, core(act_basis)], axis=1)
    grads_rot = jnp.concatenate([grad_basis, core(grad_basis)], axis=0)
    eig_oth = core(eigenvalues)

    def part_of(s):
        return jnp.dot(grads_in[s][:m], grads_rot, preferred_element_type=F32).astype(BF)

    order = []
    for k in range(n):
        mine = [(0, 0, k)]
        for d in range(1, n):
            if k - d >= 0:
                mine.append((1, d, k - d))
            if k + d < n:
                mine.append((-1, d, k + d))
        order.append(mine)

    def acts_of(a):
        buffers = [(up if order[k][a][0] >= 0 else down)[order[k][a][1]] for k in range(n)]
        x = choose(z, buffers)
        return jnp.dot(x, acts_rot, preferred_element_type=F32).astype(BF)

    parts = {0: part_of(0)}
    first_acts = {0: acts_of(0), 1: acts_of(1)}
    for level in range(2, len(bits) + 1):
        for s in range(1, R):
            if bin(s).count("1") != level:
                continue
            low, high = s & -s, 1 << (s.bit_length() - 1)
            one, two = [
                jnp.concatenate(x, axis=0) if isinstance(x, tuple) else x
                for x in (grads_in[s ^ high], grads_in[s ^ low])
            ]
            if level == 2:
                one, two = after(one, first_acts[1], parts[0]), after(two, first_acts[1], parts[0])
            one, two = one[:split], two[split:]
            first = across(one, high)
            second = across(two, low)
            grads_in[s] = (first, second)
    acts, adds = [], []
    for a in range(n):
        v = first_acts[a] if a in first_acts else acts_of(a)
        turn = a % len(bits)
        turns = bits[turn:] + bits[:turn]
        for i, b in enumerate(turns):
            got = across(v, b)
            if i < len(bits) - 1:
                v = (v.astype(F32) + got.astype(F32)).astype(BF)
        acts.append(v)
        adds.append(got)

    half_n = n // 2
    totals, inner = {}, {}

    def pairs_of(moves):
        return [(2 * k + q, 2 * l + q) for k, l in moves for q in (0, 1)]

    def add(x, y):
        return (x.astype(F32) + y.astype(F32)).astype(BF)

    for s in range(R):
        if s & (s - 1):
            pieces = [after(x, inner[s - 2]) for x in grads_in[s]]
            grads_in[s] = jnp.concatenate(pieces, axis=0)
        if s not in parts:
            parts[s] = part_of(s)
        value = parts[s]
        for j in range(half_n - 1):
            moves = pairs_of([(j, j + 1), (n - 1 - j, n - 2 - j)])
            got = lax.ppermute(value, "col", moves)
            value = add(value, got)
        inner[s] = value
        got = lax.ppermute(value, "col", pairs_of([(half_n - 1, half_n), (half_n, half_n - 1)]))
        totals[s] = [add(value, got)]
        for j in range(half_n - 1):
            moves = pairs_of([(half_n - 1 - j, half_n - 2 - j), (half_n + j, half_n + 1 + j)])
            totals[s].append(lax.ppermute(totals[s][-1], "col", moves))

    token = totals[R // 2 - 1][0]
    tg_slots = [train_grads]
    for b in range(n.bit_length() - 1):
        pairs = pairs_of([(k, k ^ (1 << b)) for k in range(n)])
        got = lax.ppermute(jnp.concatenate(tg_slots, axis=0), "col", pairs)
        got = after(got, inner[0] if b < n.bit_length() - 2 else token)
        tg_slots += [got[k * part_tg : (k + 1) * part_tg] for k in range(1 << b)]
    tg_mine = [choose(z, [tg_slots[k ^ j] for j in range(n)]) for k in range(n)]
    tg_mine = jnp.stack(tg_mine)
    tg_oth = core(tg_mine)
    tg = jnp.stack([jnp.where(p == 0, tg_mine, tg_oth), jnp.where(p == 0, tg_oth, tg_mine)], axis=1)
    tg = tg.reshape(train, tg.shape[-1])
    width = train_acts.shape[1]
    sides = [after(grads_in[k], token)[m:] for k in range(R)]
    ta = []
    for b in range(R):
        side = choose(r, [sides[b ^ k] for k in range(R)])
        ta.extend([side[:, :width], side[:, width:]])
    ta_own = jnp.concatenate(ta, axis=0)
    ta_oth = core(ta_own)

    place = [[None] * n for _ in range(n)]
    for k in range(n):
        for a in range(n):
            place[k][order[k][a][2]] = jnp.int32(a)
    pick = [z.astype(jnp.int32)]
    for s in range(R):
        pick.append(choose(z, [choose(r, [place[k][j ^ s] for j in range(R)]) for k in range(n)]))
    pick = jnp.stack(pick)

    source_of = [half_n - 1 - k if k < half_n else k - half_n for k in range(n)]
    outs = []
    for s in range(R):
        outs.append(
            chunk_scores(
                pick,
                source_of,
                s,
                totals[s],
                acts,
                adds,
                eigenvalues,
                eig_oth,
                tg,
                ta_own,
                ta_oth,
            )
        )
    slot_scores = [out[0] for out in outs]
    by_slot = jnp.stack(slot_scores)
    by_chunk = jnp.stack([choose(r, [by_slot[k ^ j] for j in range(R)]) for k in range(n)])
    share = train // (R * C)
    blocks = (by_chunk / D).reshape(n, R * C, share).transpose(1, 0, 2)
    got = lax.all_to_all(blocks, ("row", "col"), 0, 0, tiled=True)
    value = got.reshape(R * n, 2, n, share).sum(0).transpose(1, 0, 2)
    queries = C * m // QUERY_LEN
    return value.reshape(queries, 2 * n // queries, share).sum(1)


def solution(mesh):
    R, C = mesh.shape["row"], mesh.shape["col"]

    def body(*arrays):
        return shards(R, C, *arrays)

    return jax.shard_map(
        body,
        mesh=mesh,
        in_specs=(
            P("col", "row"),
            P("row", "col"),
            P("row", "col"),
            P("col", "row"),
            P("row", "col"),
            P("row", "col"),
            P("col", "row"),
        ),
        out_specs=P(None, ("row", "col")),
        check_vma=False,
    )
```

```python
import functools
import math

import jax
import jax.numpy as jnp
from jax import lax
from jax.experimental import pallas as pl
from jax.experimental.pallas import tpu as pltpu
from jax.sharding import PartitionSpec as P


D = 6144
QUERY_LEN = 256
damping = 0.01


BF = jnp.bfloat16
F32 = jnp.float32


def choose(index, options):
    out = options[-1]
    for k in range(len(options) - 2, -1, -1):
        if options[k] is not out:
            out = jnp.where(index == k, options[k], out)
    return out


def after(x, *tokens):
    return lax.optimization_barrier((x,) + tokens)[0]


def panel_kernel(tables, pick_ref, *refs):
    source_of, chunk, n_acts = tables
    n_grads = max(source_of) + 1
    grads, refs = refs[:n_grads], refs[n_grads:]
    acts, refs = refs[:n_acts], refs[n_acts:]
    adds, refs = refs[:n_acts], refs[n_acts:]
    eig_own, eig_oth, tg_ref, ta_own, ta_oth, out_ref = refs[:6]
    buf, acts_buf, acc, sems = refs[6:]
    step = pl.program_id(0)

    @pl.when(step == 0)
    def _():
        acc[...] = jnp.zeros_like(acc)
        z, at = pick_ref[0], pick_ref[1 + chunk]
        for d in range(n_grads):
            here = functools.reduce(
                jnp.logical_or, [z == k for k in range(len(source_of)) if source_of[k] == d]
            )

            @pl.when(here)
            def _(src=grads[d]):
                pltpu.make_async_copy(src, buf, sems.at[0]).start()

        for k in range(n_acts):

            @pl.when(at == k)
            def _(src=acts[k]):
                pltpu.make_async_copy(src, acts_buf.at[0], sems.at[1]).start()

            @pl.when(at == k)
            def _(src=adds[k]):
                pltpu.make_async_copy(src, acts_buf.at[1], sems.at[2]).start()

        pltpu.make_async_copy(grads[0], buf, sems.at[0]).wait()
        pltpu.make_async_copy(acts[0], acts_buf.at[0], sems.at[1]).wait()
        pltpu.make_async_copy(acts[0], acts_buf.at[1], sems.at[2]).wait()
        acts_buf[0] = (acts_buf[0].astype(F32) + acts_buf[1].astype(F32)).astype(BF)

    cols = eig_own.shape[1]
    half = acts_buf.shape[2] // 2
    total = None
    for first, eig, ta in ((0, eig_own, ta_own), (half, eig_oth, ta_oth)):
        at_col = pl.multiple_of(first + step * cols, 128)
        outer = lax.dot_general(
            buf[...],
            acts_buf[0, :, pl.ds(at_col, cols)],
            (((0,), (0,)), ((), ())),
            preferred_element_type=F32,
        )
        panel = (outer / (QUERY_LEN * (eig[...] + damping))).astype(BF)
        mapped = jnp.dot(tg_ref[...], panel, preferred_element_type=F32)
        prod = mapped * ta[...].astype(F32)
        for q in range(cols // 128):
            piece = prod[:, q * 128 : (q + 1) * 128]
            total = piece if total is None else total + piece
    acc[...] += total

    @pl.when(step == pl.num_programs(0) - 1)
    def _():
        out_ref[...] = lax.dot_general(
            jnp.ones((8, 128), F32),
            acc[...],
            (((1,), (1,)), ((), ())),
            precision=lax.Precision.HIGHEST,
            preferred_element_type=F32,
        )


def chunk_scores(pick, source_of, chunk, grads, acts, adds, eig_own, eig_oth, tg, ta_own, ta_oth):
    rows, half = eig_own.shape
    train = tg.shape[0]
    cols = math.gcd(half, 256)
    anywhere = pl.BlockSpec(memory_space=pl.ANY)
    return pl.pallas_call(
        functools.partial(
            panel_kernel,
            (source_of, chunk, len(acts)),
        ),
        out_shape=jax.ShapeDtypeStruct((8, train), F32),
        grid_spec=pltpu.PrefetchScalarGridSpec(
            num_scalar_prefetch=1,
            grid=(half // cols,),
            in_specs=[anywhere] * (len(grads) + 2 * len(acts))
            + [
                pl.BlockSpec((rows, cols), lambda j, _: (0, j)),
                pl.BlockSpec((rows, cols), lambda j, _: (0, j)),
                pl.BlockSpec((train, rows), lambda j, _: (0, 0), pipeline_mode=pl.Buffered(1)),
                pl.BlockSpec((train, cols), lambda j, _: (0, j)),
                pl.BlockSpec((train, cols), lambda j, _: (0, j)),
            ],
            out_specs=pl.BlockSpec((8, train), lambda j, _: (0, 0)),
            scratch_shapes=[
                pltpu.VMEM(grads[0].shape, BF),
                pltpu.VMEM((2,) + acts[0].shape, BF),
                pltpu.VMEM((train, 128), F32),
                pltpu.SemaphoreType.DMA((3,)),
            ],
        ),
        compiler_params=pltpu.CompilerParams(vmem_limit_bytes=18 << 20),
        cost_estimate=pl.CostEstimate(
            flops=4 * rows * half * (grads[0].shape[0] + train),
            bytes_accessed=8 * rows * half,
            transcendentals=0,
        ),
    )(pick, *grads, *acts, *adds, eig_own, eig_oth, tg, ta_own, ta_oth)


def shards(R, C, query_acts, query_grads, act_basis, grad_basis, eigenvalues, train_acts, train_grads):
    n = C // 2
    assert n == R and R & (R - 1) == 0
    r = lax.axis_index("row")
    c = lax.axis_index("col")
    z, p = c // 2, c % 2

    def core(x):
        return lax.ppermute(x, "col", [(k, k ^ 1) for k in range(C)])

    def across(x, d):
        return lax.ppermute(x, "row", [(k, k ^ d) for k in range(R)])

    def along(x, step, senders):
        pairs = [(2 * k + q, 2 * (k + step) + q) for k in senders for q in (0, 1)]
        return lax.ppermute(x, "col", pairs)

    m = query_acts.shape[0]
    part_tg = train_grads.shape[0]
    part_ta = train_acts.shape[0]
    train = part_tg * C

    packet = jnp.concatenate([query_acts, train_grads], axis=0)
    up, down = {0: packet}, {0: packet}
    for d in range(1, n):
        up[d] = along(up[d - 1], 1, range(d - 1, n - 1))
        down[d] = along(down[d - 1], -1, range(1, n - d + 1))

    halves = query_grads.reshape(2, m, query_grads.shape[1])
    keep = jnp.where(p == 0, halves[0], halves[1])
    send = jnp.where(p == 0, halves[1], halves[0])
    half_ta = part_ta // 2
    side = jnp.concatenate([train_acts[:half_ta], train_acts[half_ta:]], axis=1)
    mine = jnp.concatenate([keep, core(send)], axis=1)
    mine = jnp.concatenate([mine, side], axis=0)
    height = mine.shape[0]
    split = height // 16 * 8
    grads_in = {0: mine}
    bits = [1 << b for b in range(R.bit_length() - 1)]
    for bit in bits:
        grads_in[bit] = across(mine, bit)

    acts_rot = jnp.concatenate([act_basis, core(act_basis)], axis=1)
    grads_rot = jnp.concatenate([grad_basis, core(grad_basis)], axis=0)
    eig_oth = core(eigenvalues)

    def part_of(s):
        return jnp.dot(grads_in[s][:m], grads_rot, preferred_element_type=F32).astype(BF)

    order = []
    for k in range(n):
        mine = [(0, 0, k)]
        for d in range(1, n):
            if k - d >= 0:
                mine.append((1, d, k - d))
            if k + d < n:
                mine.append((-1, d, k + d))
        order.append(mine)

    place = [[None] * n for _ in range(n)]
    for k in range(n):
        for a in range(n):
            place[k][order[k][a][2]] = jnp.int32(a)
    pick = [z.astype(jnp.int32)]
    for s in range(R):
        pick.append(choose(z, [choose(r, [place[k][j ^ s] for j in range(R)]) for k in range(n)]))
    pick = jnp.stack(pick)

    def acts_of(a):
        buffers = [(up if order[k][a][0] >= 0 else down)[order[k][a][1]] for k in range(n)]
        x = choose(z, [x[:m] for x in buffers]) if a else after(query_acts, pick)
        return jnp.dot(x, acts_rot, preferred_element_type=F32).astype(BF)

    parts = {0: part_of(0)}
    first_acts = {0: acts_of(0), 1: acts_of(1)}
    for level in range(2, len(bits) + 1):
        for s in range(1, R):
            if bin(s).count("1") != level:
                continue
            low, high = s & -s, 1 << (s.bit_length() - 1)
            one, two = [
                jnp.concatenate(x, axis=0) if isinstance(x, tuple) else x
                for x in (grads_in[s ^ high], grads_in[s ^ low])
            ]
            if level == 2:
                one, two = after(one, first_acts[1], parts[0]), after(two, first_acts[1], parts[0])
            one, two = one[:split], two[split:]
            first = across(one, high)
            second = across(two, low)
            grads_in[s] = (first, second)
    acts, adds = [], []
    for a in range(n):
        v = first_acts[a] if a in first_acts else acts_of(a)
        turn = a % len(bits)
        turns = bits[turn:] + bits[:turn]
        for i, b in enumerate(turns):
            got = across(v, b)
            if i < len(bits) - 1:
                v = (v.astype(F32) + got.astype(F32)).astype(BF)
        acts.append(v)
        adds.append(got)

    half_n = n // 2
    totals, inner = {}, {}

    def pairs_of(moves):
        return [(2 * k + q, 2 * l + q) for k, l in moves for q in (0, 1)]

    def add(x, y):
        return (x.astype(F32) + y.astype(F32)).astype(BF)

    for s in range(R):
        if s & (s - 1):
            pieces = [after(x, inner[s - 2]) for x in grads_in[s]]
            grads_in[s] = jnp.concatenate(pieces, axis=0)
        if s not in parts:
            parts[s] = part_of(s)
        value = parts[s]
        for j in range(half_n - 1):
            moves = pairs_of([(j, j + 1), (n - 1 - j, n - 2 - j)])
            got = lax.ppermute(value, "col", moves)
            value = add(value, got)
        inner[s] = value
        got = lax.ppermute(value, "col", pairs_of([(half_n - 1, half_n), (half_n, half_n - 1)]))
        totals[s] = [add(value, got)]
        for j in range(half_n - 1):
            moves = pairs_of([(half_n - 1 - j, half_n - 2 - j), (half_n + j, half_n + 1 + j)])
            totals[s].append(lax.ppermute(totals[s][-1], "col", moves))

    token = totals[R // 2 - 1][0]
    tg_up = {k: after(up[k], token)[m:] if k else train_grads for k in up}
    tg_down = {k: after(down[k], token)[m:] for k in down if k > 0}
    tg_mine = []
    for k in range(n):
        options = [(tg_up[j - k] if j >= k else tg_down[k - j]) for j in range(n)]
        tg_mine.append(choose(z, options))
    tg_mine = jnp.stack(tg_mine)
    tg_oth = core(tg_mine)
    tg = [jnp.where(p == 0, tg_mine, tg_oth), jnp.where(p == 0, tg_oth, tg_mine)]
    tg = jnp.stack(tg, axis=1).reshape(train, tg_mine.shape[-1])
    width = train_acts.shape[1]
    sides = [after(grads_in[k], token)[m:] for k in range(R)]
    ta = []
    for b in range(R):
        side = choose(r, [sides[b ^ k] for k in range(R)])
        ta.extend([side[:, :width], side[:, width:]])
    ta_own = jnp.concatenate(ta, axis=0)
    ta_oth = core(ta_own)


    source_of = [half_n - 1 - k if k < half_n else k - half_n for k in range(n)]
    outs = []
    for s in range(R):
        outs.append(
            chunk_scores(
                pick,
                source_of,
                s,
                totals[s],
                acts,
                adds,
                eigenvalues,
                eig_oth,
                tg,
                ta_own,
                ta_oth,
            )
        )
    slot_scores = [out[0] for out in outs]
    by_slot = jnp.stack(slot_scores)
    by_chunk = jnp.stack([choose(r, [by_slot[k ^ j] for j in range(R)]) for k in range(n)])
    share = train // (R * C)
    blocks = (by_chunk / D).reshape(n, R * C, share).transpose(1, 0, 2)
    got = lax.all_to_all(blocks, ("row", "col"), 0, 0, tiled=True)
    value = got.reshape(R * n, 2, n, share).sum(0).transpose(1, 0, 2)
    queries = C * m // QUERY_LEN
    return value.reshape(queries, 2 * n // queries, share).sum(1)


def solution(mesh):
    R, C = mesh.shape["row"], mesh.shape["col"]

    def body(*arrays):
        return shards(R, C, *arrays)

    return jax.shard_map(
        body,
        mesh=mesh,
        in_specs=(
            P("col", "row"),
            P("row", "col"),
            P("row", "col"),
            P("col", "row"),
            P("row", "col"),
            P("row", "col"),
            P("col", "row"),
        ),
        out_specs=P(None, ("row", "col")),
        check_vma=False,
    )
```

```python
import functools
import math

import jax
import jax.numpy as jnp
from jax import lax
from jax.experimental import pallas as pl
from jax.experimental.pallas import tpu as pltpu
from jax.sharding import PartitionSpec as P


D = 6144
QUERY_LEN = 256
damping = 0.01


BF = jnp.bfloat16
F32 = jnp.float32


def choose(index, options):
    out = options[-1]
    for k in range(len(options) - 2, -1, -1):
        if options[k] is not out:
            out = jnp.where(index == k, options[k], out)
    return out


def after(x, *tokens):
    return lax.optimization_barrier((x,) + tokens)[0]


def panel_kernel(tables, pick_ref, *refs):
    source_of, chunk, n_acts = tables
    n_grads = max(source_of) + 1
    grads, refs = refs[:n_grads], refs[n_grads:]
    acts, refs = refs[:n_acts], refs[n_acts:]
    adds, refs = refs[:n_acts], refs[n_acts:]
    eig_own, eig_oth, tg_ref, ta_own, ta_oth, out_ref = refs[:6]
    buf, acts_buf, acc, sems = refs[6:]
    step = pl.program_id(0)

    @pl.when(step == 0)
    def _():
        acc[...] = jnp.zeros_like(acc)
        z, at = pick_ref[0], pick_ref[1 + chunk]
        for d in range(n_grads):
            here = functools.reduce(
                jnp.logical_or, [z == k for k in range(len(source_of)) if source_of[k] == d]
            )

            @pl.when(here)
            def _(src=grads[d]):
                pltpu.make_async_copy(src, buf, sems.at[0]).start()

        for k in range(n_acts):

            @pl.when(at == k)
            def _(src=acts[k]):
                pltpu.make_async_copy(src, acts_buf.at[0], sems.at[1]).start()

            @pl.when(at == k)
            def _(src=adds[k]):
                pltpu.make_async_copy(src, acts_buf.at[1], sems.at[2]).start()

        pltpu.make_async_copy(grads[0], buf, sems.at[0]).wait()
        pltpu.make_async_copy(acts[0], acts_buf.at[0], sems.at[1]).wait()
        pltpu.make_async_copy(acts[0], acts_buf.at[1], sems.at[2]).wait()
        acts_buf[0] = (acts_buf[0].astype(F32) + acts_buf[1].astype(F32)).astype(BF)

    cols = eig_own.shape[1]
    half = acts_buf.shape[2] // 2
    total = None
    for first, eig, ta in ((0, eig_own, ta_own), (half, eig_oth, ta_oth)):
        at_col = pl.multiple_of(first + step * cols, 128)
        outer = lax.dot_general(
            buf[...],
            acts_buf[0, :, pl.ds(at_col, cols)],
            (((0,), (0,)), ((), ())),
            preferred_element_type=F32,
        )
        panel = (outer / (QUERY_LEN * (eig[...] + damping))).astype(BF)
        mapped = jnp.dot(tg_ref[...], panel, preferred_element_type=F32)
        prod = mapped * ta[...].astype(F32)
        for q in range(cols // 128):
            piece = prod[:, q * 128 : (q + 1) * 128]
            total = piece if total is None else total + piece
    acc[...] += total

    @pl.when(step == pl.num_programs(0) - 1)
    def _():
        out_ref[...] = lax.dot_general(
            jnp.ones((8, 128), F32),
            acc[...],
            (((1,), (1,)), ((), ())),
            precision=lax.Precision.HIGHEST,
            preferred_element_type=F32,
        )


def chunk_scores(pick, source_of, chunk, part, grads, acts, adds, eig_own, eig_oth, tg, ta_own, ta_oth):
    rows, half = grads[0].shape[1], eig_own.shape[1]
    train = tg.shape[0]
    cols = math.gcd(half, 256)
    anywhere = pl.BlockSpec(memory_space=pl.ANY)
    return pl.pallas_call(
        functools.partial(
            panel_kernel,
            (source_of, chunk, len(acts)),
        ),
        out_shape=jax.ShapeDtypeStruct((8, train), F32),
        grid_spec=pltpu.PrefetchScalarGridSpec(
            num_scalar_prefetch=1,
            grid=(half // cols,),
            in_specs=[anywhere] * (len(grads) + 2 * len(acts))
            + [
                pl.BlockSpec((rows, cols), lambda j, _: (part, j)),
                pl.BlockSpec((rows, cols), lambda j, _: (part, j)),
                pl.BlockSpec((train, rows), lambda j, _: (0, part), pipeline_mode=pl.Buffered(1)),
                pl.BlockSpec((train, cols), lambda j, _: (0, j)),
                pl.BlockSpec((train, cols), lambda j, _: (0, j)),
            ],
            out_specs=pl.BlockSpec((8, train), lambda j, _: (0, 0)),
            scratch_shapes=[
                pltpu.VMEM(grads[0].shape, BF),
                pltpu.VMEM((2,) + acts[0].shape, BF),
                pltpu.VMEM((train, 128), F32),
                pltpu.SemaphoreType.DMA((3,)),
            ],
        ),
        compiler_params=pltpu.CompilerParams(vmem_limit_bytes=18 << 20),
        cost_estimate=pl.CostEstimate(
            flops=4 * rows * half * (grads[0].shape[0] + train),
            bytes_accessed=8 * rows * half,
            transcendentals=0,
        ),
    )(pick, *grads, *acts, *adds, eig_own, eig_oth, tg, ta_own, ta_oth)


def shards(R, C, query_acts, query_grads, act_basis, grad_basis, eigenvalues, train_acts, train_grads):
    n = C // 2
    assert n == R and R & (R - 1) == 0
    r = lax.axis_index("row")
    c = lax.axis_index("col")
    z, p = c // 2, c % 2

    def core(x):
        return lax.ppermute(x, "col", [(k, k ^ 1) for k in range(C)])

    def across(x, d):
        return lax.ppermute(x, "row", [(k, k ^ d) for k in range(R)])

    def along(x, step, senders):
        pairs = [(2 * k + q, 2 * (k + step) + q) for k in senders for q in (0, 1)]
        return lax.ppermute(x, "col", pairs)

    m = query_acts.shape[0]
    part_tg = train_grads.shape[0]
    part_ta = train_acts.shape[0]
    train = part_tg * C

    up, down = {0: query_acts}, {0: query_acts}
    tg_up, tg_down = {0: train_grads}, {0: train_grads}
    for d in range(1, n):
        going_up, going_down = range(d - 1, n - 1), range(1, n - d + 1)
        up[d] = along(up[d - 1], 1, going_up)
        down[d] = along(down[d - 1], -1, going_down)
        tg_up[d] = along(tg_up[d - 1], 1, going_up)
        tg_down[d] = along(tg_down[d - 1], -1, going_down)

    halves = query_grads.reshape(2, m, query_grads.shape[1])
    keep = jnp.where(p == 0, halves[0], halves[1])
    send = jnp.where(p == 0, halves[1], halves[0])
    half_ta = part_ta // 2
    side = jnp.concatenate([train_acts[:half_ta], train_acts[half_ta:]], axis=1)
    mine = jnp.concatenate([keep, core(send)], axis=1)
    mine = jnp.concatenate([mine, side], axis=0)
    height = mine.shape[0]
    split = height // 16 * 8
    grads_in = {0: mine}
    bits = [1 << b for b in range(R.bit_length() - 1)]
    for bit in bits:
        grads_in[bit] = across(mine, bit)

    acts_rot = jnp.concatenate([act_basis, core(act_basis)], axis=1)
    grads_rot = jnp.concatenate([grad_basis, core(grad_basis)], axis=0)
    eig_oth = core(eigenvalues)

    def part_of(s):
        return jnp.dot(grads_in[s][:m], grads_rot, preferred_element_type=F32).astype(BF)

    order = []
    for k in range(n):
        mine = [(0, 0, k)]
        for d in range(1, n):
            if k - d >= 0:
                mine.append((1, d, k - d))
            if k + d < n:
                mine.append((-1, d, k + d))
        order.append(mine)

    place = [[None] * n for _ in range(n)]
    for k in range(n):
        for a in range(n):
            place[k][order[k][a][2]] = jnp.int32(a)
    pick = [z.astype(jnp.int32)]
    for s in range(R):
        pick.append(choose(z, [choose(r, [place[k][j ^ s] for j in range(R)]) for k in range(n)]))
    pick = jnp.stack(pick)

    def acts_of(a):
        buffers = [(up if order[k][a][0] >= 0 else down)[order[k][a][1]] for k in range(n)]
        x = choose(z, buffers) if a else after(query_acts, pick)
        return jnp.dot(x, acts_rot, preferred_element_type=F32).astype(BF)

    parts = {0: part_of(0)}
    first_acts = {0: acts_of(0), 1: acts_of(1)}
    for level in range(2, len(bits) + 1):
        for s in range(1, R):
            if bin(s).count("1") != level:
                continue
            low, high = s & -s, 1 << (s.bit_length() - 1)
            one, two = [
                jnp.concatenate(x, axis=0) if isinstance(x, tuple) else x
                for x in (grads_in[s ^ high], grads_in[s ^ low])
            ]
            if level == 2:
                one, two = after(one, first_acts[1], parts[0]), after(two, first_acts[1], parts[0])
            one, two = one[:split], two[split:]
            first = across(one, high)
            second = across(two, low)
            grads_in[s] = (first, second)
    acts, adds = [], []
    for a in range(n):
        v = first_acts[a] if a in first_acts else acts_of(a)
        turn = a % len(bits)
        turns = bits[turn:] + bits[:turn]
        for i, b in enumerate(turns):
            got = across(v, b)
            if i < len(bits) - 1:
                v = (v.astype(F32) + got.astype(F32)).astype(BF)
        acts.append(v)
        adds.append(got)

    half_n = n // 2
    totals, inner = {}, {}
    width = grads_rot.shape[1]

    def pairs_of(moves):
        return [(2 * k + q, 2 * l + q) for k, l in moves for q in (0, 1)]

    def add(x, y):
        return (x.astype(F32) + y.astype(F32)).astype(BF)

    for s in range(R):
        if s & (s - 1):
            pieces = [after(x, inner[s - 2]) for x in grads_in[s]]
            grads_in[s] = jnp.concatenate(pieces, axis=0)
        if s not in parts:
            parts[s] = part_of(s)
        value = parts[s]
        for j in range(half_n - 1):
            moves = pairs_of([(j, j + 1), (n - 1 - j, n - 2 - j)])
            got = lax.ppermute(value, "col", moves)
            value = add(value, got)
        inner[s] = value
        got = lax.ppermute(value, "col", pairs_of([(half_n - 1, half_n), (half_n, half_n - 1)]))
        spans = [slice(None)] if s < R - 1 else [slice(0, width // 2), slice(width // 2, width)]
        totals[s] = []
        for cols in spans:
            chain = [add(value[:, cols], got[:, cols])]
            for j in range(half_n - 1):
                moves = pairs_of([(half_n - 1 - j, half_n - 2 - j), (half_n + j, half_n + 1 + j)])
                chain.append(lax.ppermute(chain[-1], "col", moves))
            totals[s].append(chain)

    token = totals[R // 2 - 1][0][0]
    tg_up = {k: after(tg_up[k], token) if k else train_grads for k in tg_up}
    tg_down = {k: after(tg_down[k], token) for k in tg_down if k > 0}
    tg_mine = []
    for k in range(n):
        options = [(tg_up[j - k] if j >= k else tg_down[k - j]) for j in range(n)]
        tg_mine.append(choose(z, options))
    tg_mine = jnp.stack(tg_mine)
    tg_oth = core(tg_mine)
    tg = [jnp.where(p == 0, tg_mine, tg_oth), jnp.where(p == 0, tg_oth, tg_mine)]
    tg = jnp.stack(tg, axis=1).reshape(train, tg_mine.shape[-1])
    cols = train_acts.shape[1]
    sides = [after(grads_in[k], token)[m:] for k in range(R)]
    ta = []
    for b in range(R):
        side = choose(r, [sides[b ^ k] for k in range(R)])
        ta.extend([side[:, :cols], side[:, cols:]])
    ta_own = jnp.concatenate(ta, axis=0)
    ta_oth = core(ta_own)


    source_of = [half_n - 1 - k if k < half_n else k - half_n for k in range(n)]
    outs = []
    for s in range(R):
        out = None
        for h, chain in enumerate(totals[s]):
            piece = chunk_scores(
                pick,
                source_of,
                s,
                h,
                chain,
                acts,
                adds,
                eigenvalues,
                eig_oth,
                tg,
                ta_own,
                ta_oth,
            )
            out = piece if out is None else out + piece
        outs.append(out)
    slot_scores = [out[0] for out in outs]
    by_slot = jnp.stack(slot_scores)
    by_chunk = jnp.stack([choose(r, [by_slot[k ^ j] for j in range(R)]) for k in range(n)])
    share = train // (R * C)
    blocks = (by_chunk / D).reshape(n, R * C, share).transpose(1, 0, 2)
    got = lax.all_to_all(blocks, ("row", "col"), 0, 0, tiled=True)
    value = got.reshape(R * n, 2, n, share).sum(0).transpose(1, 0, 2)
    queries = C * m // QUERY_LEN
    return value.reshape(queries, 2 * n // queries, share).sum(1)


def solution(mesh):
    R, C = mesh.shape["row"], mesh.shape["col"]

    def body(*arrays):
        return shards(R, C, *arrays)

    return jax.shard_map(
        body,
        mesh=mesh,
        in_specs=(
            P("col", "row"),
            P("row", "col"),
            P("row", "col"),
            P("col", "row"),
            P("row", "col"),
            P("row", "col"),
            P("col", "row"),
        ),
        out_specs=P(None, ("row", "col")),
        check_vma=False,
    )
```

```python
import functools
import math

import jax
import jax.numpy as jnp
from jax import lax
from jax.experimental import pallas as pl
from jax.experimental.pallas import tpu as pltpu
from jax.sharding import PartitionSpec as P


D = 6144
QUERY_LEN = 256
damping = 0.01


BF = jnp.bfloat16
F32 = jnp.float32


def choose(index, options):
    out = options[-1]
    for k in range(len(options) - 2, -1, -1):
        if options[k] is not out:
            out = jnp.where(index == k, options[k], out)
    return out


def after(x, *tokens):
    return lax.optimization_barrier((x,) + tokens)[0]


def panel_kernel(tables, pick_ref, *refs):
    source_of, chunk, n_acts = tables
    n_grads = max(source_of) + 1
    grads, refs = refs[:n_grads], refs[n_grads:]
    acts, refs = refs[:n_acts], refs[n_acts:]
    adds, refs = refs[:n_acts], refs[n_acts:]
    eig_own, eig_oth, tg_ref, ta_own, ta_oth, out_ref = refs[:6]
    buf, acts_buf, acc, sems = refs[6:]
    z, at = pick_ref[0], pick_ref[1 + chunk]
    for d in range(n_grads):
        here = functools.reduce(
            jnp.logical_or, [z == k for k in range(len(source_of)) if source_of[k] == d]
        )

        @pl.when(here)
        def _(src=grads[d]):
            pltpu.make_async_copy(src, buf, sems.at[0]).start()

    for k in range(n_acts):

        @pl.when(at == k)
        def _(k=k):
            pltpu.make_async_copy(acts[k], acts_buf.at[0], sems.at[1]).start()
            pltpu.make_async_copy(adds[k], acts_buf.at[1], sems.at[2]).start()

    pltpu.make_async_copy(grads[0], buf, sems.at[0]).wait()
    pltpu.make_async_copy(acts[0], acts_buf.at[0], sems.at[1]).wait()
    pltpu.make_async_copy(adds[0], acts_buf.at[1], sems.at[2]).wait()
    acts_buf[0] = (acts_buf[0].astype(F32) + acts_buf[1].astype(F32)).astype(BF)

    half = acts_buf.shape[2] // 2
    tile = math.gcd(half, 256)
    acc[...] = jnp.zeros_like(acc)

    def tile_scores(i, carry):
        total = None
        col = pl.multiple_of(i * tile, 128)
        for first, eig, ta in ((0, eig_own, ta_own), (half, eig_oth, ta_oth)):
            outer = lax.dot_general(
                buf[...],
                acts_buf[0, :, pl.ds(pl.multiple_of(first + i * tile, 128), tile)],
                (((0,), (0,)), ((), ())),
                preferred_element_type=F32,
            )
            scale = QUERY_LEN * (eig[:, pl.ds(col, tile)] + damping)
            panel = (outer / scale).astype(BF)
            mapped = jnp.dot(tg_ref[...], panel, preferred_element_type=F32)
            prod = mapped * ta[:, pl.ds(col, tile)].astype(F32)
            for q in range(0, tile, 128):
                piece = prod[:, q : q + 128]
                total = piece if total is None else total + piece
        acc[...] += total
        return carry

    lax.fori_loop(0, half // tile, tile_scores, 0)
    out_ref[...] = lax.dot_general(
        jnp.ones((8, 128), F32),
        acc[...],
        (((1,), (1,)), ((), ())),
        precision=lax.Precision.HIGHEST,
        preferred_element_type=F32,
    )


def chunk_scores(pick, source_of, chunk, part, grads, acts, adds, eig_own, eig_oth, tg, ta_own, ta_oth):
    rows, half = grads[0].shape[1], eig_own.shape[1]
    train = tg.shape[0]
    anywhere = pl.BlockSpec(memory_space=pl.ANY)
    return pl.pallas_call(
        functools.partial(
            panel_kernel,
            (source_of, chunk, len(acts)),
        ),
        out_shape=jax.ShapeDtypeStruct((8, train), F32),
        grid_spec=pltpu.PrefetchScalarGridSpec(
            num_scalar_prefetch=1,
            grid=(1,),
            in_specs=[anywhere] * (len(grads) + 2 * len(acts))
            + [
                pl.BlockSpec((rows, half), lambda j, _: (part, 0)),
                pl.BlockSpec((rows, half), lambda j, _: (part, 0)),
                pl.BlockSpec((train, rows), lambda j, _: (0, part)),
                pl.BlockSpec((train, half), lambda j, _: (0, 0)),
                pl.BlockSpec((train, half), lambda j, _: (0, 0)),
            ],
            out_specs=pl.BlockSpec((8, train), lambda j, _: (0, 0)),
            scratch_shapes=[
                pltpu.VMEM(grads[0].shape, BF),
                pltpu.VMEM((2,) + acts[0].shape, BF),
                pltpu.VMEM((train, 128), F32),
                pltpu.SemaphoreType.DMA((3,)),
            ],
        ),
        compiler_params=pltpu.CompilerParams(vmem_limit_bytes=22 << 20),
        cost_estimate=pl.CostEstimate(
            flops=4 * rows * half * (grads[0].shape[0] + train),
            bytes_accessed=8 * rows * half,
            transcendentals=0,
        ),
    )(pick, *grads, *acts, *adds, eig_own, eig_oth, tg, ta_own, ta_oth)


def shards(R, C, query_acts, query_grads, act_basis, grad_basis, eigenvalues, train_acts, train_grads):
    n = C // 2
    assert n == R and R & (R - 1) == 0
    r = lax.axis_index("row")
    c = lax.axis_index("col")
    z, p = c // 2, c % 2

    def core(x):
        return lax.ppermute(x, "col", [(k, k ^ 1) for k in range(C)])

    def across(x, d):
        return lax.ppermute(x, "row", [(k, k ^ d) for k in range(R)])

    def along(x, step, senders):
        pairs = [(2 * k + q, 2 * (k + step) + q) for k in senders for q in (0, 1)]
        return lax.ppermute(x, "col", pairs)

    m = query_acts.shape[0]
    part_tg = train_grads.shape[0]
    part_ta = train_acts.shape[0]
    train = part_tg * C

    packet = jnp.concatenate([query_acts, train_grads], axis=0)
    up, down = {0: packet}, {0: packet}
    for d in range(1, n):
        up[d] = along(up[d - 1], 1, range(d - 1, n - 1))
        down[d] = along(down[d - 1], -1, range(1, n - d + 1))

    halves = query_grads.reshape(2, m, query_grads.shape[1])
    keep = jnp.where(p == 0, halves[0], halves[1])
    send = jnp.where(p == 0, halves[1], halves[0])
    half_ta = part_ta // 2
    side = jnp.concatenate([train_acts[:half_ta], train_acts[half_ta:]], axis=1)
    mine = jnp.concatenate([keep, core(send)], axis=1)
    mine = jnp.concatenate([mine, side], axis=0)
    height = mine.shape[0]
    split = height // 16 * 8
    grads_in = {0: mine}
    bits = [1 << b for b in range(R.bit_length() - 1)]
    for bit in bits:
        grads_in[bit] = across(mine, bit)

    acts_rot = jnp.concatenate([act_basis, core(act_basis)], axis=1)
    grads_rot = jnp.concatenate([grad_basis, core(grad_basis)], axis=0)
    eig_oth = core(eigenvalues)

    def part_of(s):
        return jnp.dot(grads_in[s][:m], grads_rot, preferred_element_type=F32).astype(BF)

    order = []
    for k in range(n):
        mine = [(0, 0, k)]
        for d in range(1, n):
            if k - d >= 0:
                mine.append((1, d, k - d))
            if k + d < n:
                mine.append((-1, d, k + d))
        order.append(mine)

    place = [[None] * n for _ in range(n)]
    for k in range(n):
        for a in range(n):
            place[k][order[k][a][2]] = jnp.int32(a)
    pick = [z.astype(jnp.int32)]
    for s in range(R):
        pick.append(choose(z, [choose(r, [place[k][j ^ s] for j in range(R)]) for k in range(n)]))
    pick = jnp.stack(pick)

    def acts_of(a):
        buffers = [(up if order[k][a][0] >= 0 else down)[order[k][a][1]] for k in range(n)]
        x = choose(z, [x[:m] for x in buffers]) if a else after(query_acts, pick)
        return jnp.dot(x, acts_rot, preferred_element_type=F32).astype(BF)

    parts = {0: part_of(0)}
    first_acts = {0: acts_of(0), 1: acts_of(1)}
    for level in range(2, len(bits) + 1):
        for s in range(1, R):
            if bin(s).count("1") != level:
                continue
            low, high = s & -s, 1 << (s.bit_length() - 1)
            one, two = [
                jnp.concatenate(x, axis=0) if isinstance(x, tuple) else x
                for x in (grads_in[s ^ high], grads_in[s ^ low])
            ]
            if level == 2:
                one, two = after(one, first_acts[1], parts[0]), after(two, first_acts[1], parts[0])
            one, two = one[:split], two[split:]
            first = across(one, high)
            second = across(two, low)
            grads_in[s] = (first, second)
    acts, adds = [], []
    for a in range(n):
        v = first_acts[a] if a in first_acts else acts_of(a)
        turn = a % len(bits)
        turns = bits[turn:] + bits[:turn]
        for i, b in enumerate(turns):
            got = across(v, b)
            if i < len(bits) - 1:
                v = (v.astype(F32) + got.astype(F32)).astype(BF)
        acts.append(v)
        adds.append(got)

    half_n = n // 2
    totals, inner = {}, {}
    width = grads_rot.shape[1]

    def pairs_of(moves):
        return [(2 * k + q, 2 * l + q) for k, l in moves for q in (0, 1)]

    def add(x, y):
        return (x.astype(F32) + y.astype(F32)).astype(BF)

    for s in range(R):
        if s & (s - 1):
            pieces = [after(x, inner[s - 2]) for x in grads_in[s]]
            grads_in[s] = jnp.concatenate(pieces, axis=0)
        if s not in parts:
            parts[s] = part_of(s)
        value = parts[s]
        for j in range(half_n - 1):
            moves = pairs_of([(j, j + 1), (n - 1 - j, n - 2 - j)])
            got = lax.ppermute(value, "col", moves)
            value = add(value, got)
        inner[s] = value
        got = lax.ppermute(value, "col", pairs_of([(half_n - 1, half_n), (half_n, half_n - 1)]))
        spans = [slice(None)] if s < R - 1 else [slice(0, width // 2), slice(width // 2, width)]
        totals[s] = []
        for cols in spans:
            chain = [add(value[:, cols], got[:, cols])]
            for j in range(half_n - 1):
                moves = pairs_of([(half_n - 1 - j, half_n - 2 - j), (half_n + j, half_n + 1 + j)])
                chain.append(lax.ppermute(chain[-1], "col", moves))
            totals[s].append(chain)

    token = totals[R // 2 - 1][0][0]
    tg_up = {k: after(up[k], token)[m:] if k else train_grads for k in up}
    tg_down = {k: after(down[k], token)[m:] for k in down if k > 0}
    tg_mine = []
    for k in range(n):
        options = [(tg_up[j - k] if j >= k else tg_down[k - j]) for j in range(n)]
        tg_mine.append(choose(z, options))
    tg_mine = jnp.stack(tg_mine)
    tg_oth = core(tg_mine)
    tg = [jnp.where(p == 0, tg_mine, tg_oth), jnp.where(p == 0, tg_oth, tg_mine)]
    tg = jnp.stack(tg, axis=1).reshape(train, tg_mine.shape[-1])
    cols = train_acts.shape[1]
    sides = [after(grads_in[k], token)[m:] for k in range(R)]
    ta = []
    for b in range(R):
        side = choose(r, [sides[b ^ k] for k in range(R)])
        ta.extend([side[:, :cols], side[:, cols:]])
    ta_own = jnp.concatenate(ta, axis=0)
    ta_oth = core(ta_own)


    source_of = [half_n - 1 - k if k < half_n else k - half_n for k in range(n)]
    outs = []
    for s in range(R):
        out = None
        for h, chain in enumerate(totals[s]):
            piece = chunk_scores(
                pick,
                source_of,
                s,
                h,
                chain,
                acts,
                adds,
                eigenvalues,
                eig_oth,
                tg,
                ta_own,
                ta_oth,
            )
            out = piece if out is None else out + piece
        outs.append(out)
    slot_scores = [out[0] for out in outs]
    by_slot = jnp.stack(slot_scores)
    by_chunk = jnp.stack([choose(r, [by_slot[k ^ j] for j in range(R)]) for k in range(n)])
    share = train // (R * C)
    blocks = (by_chunk / D).reshape(n, R * C, share).transpose(1, 0, 2)
    got = lax.all_to_all(blocks, ("row", "col"), 0, 0, tiled=True)
    value = got.reshape(R * n, 2, n, share).sum(0).transpose(1, 0, 2)
    queries = C * m // QUERY_LEN
    return value.reshape(queries, 2 * n // queries, share).sum(1)


def solution(mesh):
    R, C = mesh.shape["row"], mesh.shape["col"]

    def body(*arrays):
        return shards(R, C, *arrays)

    return jax.shard_map(
        body,
        mesh=mesh,
        in_specs=(
            P("col", "row"),
            P("row", "col"),
            P("row", "col"),
            P("col", "row"),
            P("row", "col"),
            P("row", "col"),
            P("col", "row"),
        ),
        out_specs=P(None, ("row", "col")),
        check_vma=False,
    )
```
